32 devices in a mesh: dp: 16 (over z, x, core), seq: 2 (over y).
Axes of the slice: x: 2, y: 2, z: 4, core: 2. Of those that a mesh axis runs over, the one named last changes fastest.
Arguments:
- images: bfloat16 [32, 592, 1024], P('dp', 'seq'), may hold values from -6 to 6
- cotangent: bfloat16 [32, 592, 1024], P('dp', 'seq'), may hold values from -6 to 6
- w_qkv: float32 [1024, 3072], P('dp', 'seq'), may hold values from -0.1875 to 0.1875
- w_out: float32 [1024, 1024], P('dp', 'seq'), may hold values from -1 to 1
- w_up: float32 [1024, 4096], P('dp', 'seq'), may hold values from -0.1875 to 0.1875
- w_down: float32 [4096, 1024], P('dp', 'seq'), may hold values from -0.09375 to 0.09375
- gains: float32 [2, 1024], P(None, ('dp', 'seq')), may hold values from 0.5 to 1.5
- biases: float32 [10, 1024], P(None, ('dp', 'seq')), may hold values from -3 to 3
- first_qkv: float32 [1024, 3072], P('dp', 'seq'), may hold values from -120 to 120
- first_out: float32 [1024, 1024], P('dp', 'seq'), may hold values from -120 to 120
- first_up: float32 [1024, 4096], P('dp', 'seq'), may hold values from -120 to 120
- first_down: float32 [4096, 1024], P('dp', 'seq'), may hold values from -120 to 120
- first_gains: float32 [2, 1024], P(None, ('dp', 'seq')), may hold values from -120 to 120
- first_biases: float32 [10, 1024], P(None, ('dp', 'seq')), may hold values from -120 to 120
- second_qkv: float32 [1024, 3072], P('dp', 'seq'), may hold values from 100 to 10000
- second_out: float32 [1024, 1024], P('dp', 'seq'), may hold values from 100 to 10000
- second_up: float32 [1024, 4096], P('dp', 'seq'), may hold values from 100 to 10000
- second_down: float32 [4096, 1024], P('dp', 'seq'), may hold values from 100 to 10000
- second_gains: float32 [2, 1024], P(None, ('dp', 'seq')), may hold values from 100 to 10000
- second_biases: float32 [10, 1024], P(None, ('dp', 'seq')), may hold values from 100 to 10000
Outputs:
- out_images: bfloat16 [32, 592, 1024], P('dp', 'seq')
- grad_images: bfloat16 [32, 592, 1024], P('dp', 'seq')
- grad_qkv: float32 [1024, 3072], P('dp', 'seq')
- grad_out: float32 [1024, 1024], P('dp', 'seq')
- grad_up: float32 [1024, 4096], P('dp', 'seq')
- grad_down: float32 [4096, 1024], P('dp', 'seq')
- grad_gains: float32 [2, 1024], P(None, ('dp', 'seq'))
- grad_biases: float32 [10, 1024], P(None, ('dp', 'seq'))
- new_qkv: float32 [1024, 3072], P('dp', 'seq')
- new_out: float32 [1024, 1024], P('dp', 'seq')
- new_up: float32 [1024, 4096], P('dp', 'seq')
- new_down: float32 [4096, 1024], P('dp', 'seq')
- new_gains: float32 [2, 1024], P(None, ('dp', 'seq'))
- new_biases: float32 [10, 1024], P(None, ('dp', 'seq'))
- new_first_qkv: float32 [1024, 3072], P('dp', 'seq')
- new_first_out: float32 [1024, 1024], P('dp', 'seq')
- new_first_up: float32 [1024, 4096], P('dp', 'seq')
- new_first_down: float32 [4096, 1024], P('dp', 'seq')
- new_first_gains: float32 [2, 1024], P(None, ('dp', 'seq'))
- new_first_biases: float32 [10, 1024], P(None, ('dp', 'seq'))
- new_second_qkv: float32 [1024, 3072], P('dp', 'seq')
- new_second_out: float32 [1024, 1024], P('dp', 'seq')
- new_second_up: float32 [1024, 4096], P('dp', 'seq')
- new_second_down: float32 [4096, 1024], P('dp', 'seq')
- new_second_gains: float32 [2, 1024], P(None, ('dp', 'seq'))
- new_second_biases: float32 [10, 1024], P(None, ('dp', 'seq'))
The draws below stay inside these ranges and needn't reach their ends.
All inputs are finite; a program needn't handle non-finite values.
Results may differ from the reference program's by a relative error of at most 0.028.
Values may be sent and summed in bfloat16 or wider, within the bound.
A program may use at most 256 MiB of HBM per device.

```python
import math
import jax
import jax.numpy as jnp
from jax import lax

D = 1024
HEAD_DIM = 64
FF = 4096
PATCH_TOK = 577
STEP = 5
SEQ_PAD = 592
IMAGES = 32


def steps_of(key, shape, shards, least, high):
    factor_of, own = 1.0, jax.random.fold_in(key, 6)
    for position, parts in shards:
        heights = jnp.exp(jax.random.uniform(jax.random.fold_in(own, position), (parts,), jnp.float32, least / len(shards), high / len(shards)))
        factor_of = factor_of * jnp.repeat(heights, shape[position] // parts).reshape([-1 if axis == position else 1 for axis in range(len(shape))])
    return factor_of


def normal_values(own_key, shape, deviation, most, split=(), kind=jnp.bfloat16):
    entries = deviation * jax.random.normal(own_key, shape, jnp.float32)
    if split:
        entries = entries * steps_of(own_key, shape, split, -0.22, 0.18)
    return jnp.clip(entries, -most, most).astype(kind)


def setup_inputs(seed: int = 0) -> dict:
    splits = jax.random.split(jax.random.key(seed), 21)
    return {
        "images": normal_values(splits[0], (IMAGES, SEQ_PAD, D), 1.0, 6.0, ((0, 16), (1, 2))),
        "cotangent": normal_values(splits[1], (IMAGES, SEQ_PAD, D), 1.0, 6.0, ((0, 16), (1, 2))),
        "w_qkv": normal_values(splits[2], (D, 3 * D), D ** -0.5, 0.1875, ((0, 16), (1, 2)), jnp.float32),
        "w_out": normal_values(splits[3], (D, D), (D // 24) ** -0.5, 1.0, ((0, 16), (1, 2)), jnp.float32),
        "w_up": normal_values(splits[4], (D, FF), D ** -0.5, 0.1875, ((0, 16), (1, 2)), jnp.float32),
        "w_down": normal_values(splits[5], (FF, D), FF ** -0.5, 0.09375, ((0, 16), (1, 2)), jnp.float32),
        "gains": jnp.clip(1.0 + 0.1 * jax.random.normal(splits[6], (2, D), jnp.float32), 0.5, 1.5),
        "biases": normal_values(splits[7], (10, D), 0.5, 3.0, ((1, 32),), jnp.float32),
        "first_qkv": normal_values(splits[8], (D, 3 * D), 20.0, 120.0, ((0, 16), (1, 2)), jnp.float32),
        "first_out": normal_values(splits[9], (D, D), 20.0, 120.0, ((0, 16), (1, 2)), jnp.float32),
        "first_up": normal_values(splits[10], (D, FF), 20.0, 120.0, ((0, 16), (1, 2)), jnp.float32),
        "first_down": normal_values(splits[11], (FF, D), 20.0, 120.0, ((0, 16), (1, 2)), jnp.float32),
        "first_gains": normal_values(splits[12], (2, D), 20.0, 120.0, ((1, 32),), jnp.float32),
        "first_biases": normal_values(splits[13], (10, D), 20.0, 120.0, ((1, 32),), jnp.float32),
        "second_qkv": jnp.clip(jnp.exp(math.log(10000.0) - 4.6051702 * jax.random.uniform(splits[14], (D, 3 * D), jnp.float32) ** steps_of(splits[14], (D, 3 * D), ((0, 16), (1, 2)), -0.2, 0.2)), 100.0, 10000.0),
        "second_out": jnp.clip(jnp.exp(math.log(10000.0) - 4.6051702 * jax.random.uniform(splits[15], (D, D), jnp.float32) ** steps_of(splits[15], (D, D), ((0, 16), (1, 2)), -0.2, 0.2)), 100.0, 10000.0),
        "second_up": jnp.clip(jnp.exp(math.log(10000.0) - 4.6051702 * jax.random.uniform(splits[16], (D, FF), jnp.float32) ** steps_of(splits[16], (D, FF), ((0, 16), (1, 2)), -0.2, 0.2)), 100.0, 10000.0),
        "second_down": jnp.clip(jnp.exp(math.log(10000.0) - 4.6051702 * jax.random.uniform(splits[17], (FF, D), jnp.float32) ** steps_of(splits[17], (FF, D), ((0, 16), (1, 2)), -0.2, 0.2)), 100.0, 10000.0),
        "second_gains": jnp.clip(jnp.exp(math.log(10000.0) - 4.6051702 * jax.random.uniform(splits[18], (2, D), jnp.float32) ** steps_of(splits[18], (2, D), ((1, 32),), -0.2, 0.2)), 100.0, 10000.0),
        "second_biases": jnp.clip(jnp.exp(math.log(10000.0) - 4.6051702 * jax.random.uniform(splits[19], (10, D), jnp.float32) ** steps_of(splits[19], (10, D), ((1, 32),), -0.2, 0.2)), 100.0, 10000.0),
    }


def rounded(values):
    return lax.optimization_barrier(values.astype(jnp.bfloat16)).astype(jnp.float32)

def normalize(rows):
    center = rows - lax.optimization_barrier(jnp.mean(rows, axis=-1, keepdims=True))
    inverse = lax.rsqrt(lax.optimization_barrier(jnp.mean(center * center, axis=-1, keepdims=True)) + 1e-06)
    return (center * inverse, inverse)

def norm_back(grad_out, normed, inverse, gain):
    scaled = grad_out * gain
    return inverse * (scaled - lax.optimization_barrier(jnp.mean(scaled, axis=-1, keepdims=True)) - normed * lax.optimization_barrier(jnp.mean(scaled * normed, axis=-1, keepdims=True)))

def gelu_value(pre):
    return pre * 0.5 * (1.0 + lax.erf(pre * 0.7071067811865476))

def gelu_slope(pre):
    return 0.5 * (1.0 + lax.erf(pre * 0.7071067811865476)) + pre * jnp.exp(-0.5 * pre * pre) * 0.3989422804014327

def layer_pass(image, grad_in, kernels, live):
    w_qkv, w_out, w_up, w_down, gains, biases = kernels
    width = image.shape[-1]
    heads = width // HEAD_DIM
    scale = HEAD_DIM ** (-0.5)
    gain = gains.astype(jnp.float32)
    bias = biases.astype(jnp.float32)
    rows = image.astype(jnp.float32)
    normed_a, inverse_a = normalize(rows)
    hidden_a = (normed_a * gain[0] + bias[0]).astype(jnp.bfloat16)
    mixed = jnp.dot(hidden_a, w_qkv, preferred_element_type=jnp.float32)
    queries = (mixed[:, :width] + bias[1]).astype(jnp.bfloat16)
    keys = mixed[:, width:2 * width].astype(jnp.bfloat16)
    values = (mixed[:, 2 * width:] + bias[2]).astype(jnp.bfloat16)
    query_heads = queries.astype(jnp.float32).reshape(-1, heads, HEAD_DIM)
    key_heads = keys.astype(jnp.float32).reshape(-1, heads, HEAD_DIM)
    value_heads = values.astype(jnp.float32).reshape(-1, heads, HEAD_DIM)
    scores = jnp.einsum('chd,shd->hcs', query_heads, key_heads) * scale
    scores = jnp.where(live[None, None, :], scores, -1e+30)
    top = lax.optimization_barrier(jnp.max(scores, axis=-1, keepdims=True))
    lse = top + jnp.log(lax.optimization_barrier(jnp.sum(jnp.exp(scores - top), axis=-1, keepdims=True)))
    probs = jnp.exp(scores - lse)
    probs_b = rounded(probs)
    context = jnp.einsum('hcs,shd->chd', probs_b, value_heads).reshape(-1, width).astype(jnp.bfloat16)
    resid = rows + jnp.dot(context, w_out, preferred_element_type=jnp.float32) + bias[3]
    normed_b, inverse_b = normalize(resid)
    hidden_b = (normed_b * gain[1] + bias[4]).astype(jnp.bfloat16)
    pre = jnp.dot(hidden_b, w_up, preferred_element_type=jnp.float32) + bias[6:].reshape(-1)
    active = gelu_value(pre).astype(jnp.bfloat16)
    output = (resid + jnp.dot(active, w_down, preferred_element_type=jnp.float32) + bias[5]).astype(jnp.bfloat16)
    grad_y = grad_in.astype(jnp.float32) * live[:, None].astype(jnp.float32)
    grad_yb = grad_y.astype(jnp.bfloat16)
    g_down = jnp.dot(active.T, grad_yb, preferred_element_type=jnp.float32)
    grad_pre = jnp.dot(grad_yb, w_down.T, preferred_element_type=jnp.float32) * gelu_slope(pre)
    grad_preb = grad_pre.astype(jnp.bfloat16)
    g_up = jnp.dot(hidden_b.T, grad_preb, preferred_element_type=jnp.float32)
    grad_hb = jnp.dot(grad_preb, w_up.T, preferred_element_type=jnp.float32)
    grad_resid = grad_y + norm_back(grad_hb, normed_b, inverse_b, gain[1])
    grad_rb = grad_resid.astype(jnp.bfloat16)
    g_outw = jnp.dot(context.T, grad_rb, preferred_element_type=jnp.float32)
    grad_ctx = rounded(jnp.dot(grad_rb, w_out.T, preferred_element_type=jnp.float32)).reshape(-1, heads, HEAD_DIM)
    grad_probs = jnp.einsum('chd,shd->hcs', grad_ctx, value_heads)
    grad_vals = jnp.einsum('hcs,chd->shd', probs_b, grad_ctx).reshape(-1, width)
    delta = lax.optimization_barrier(jnp.sum(probs * grad_probs, axis=-1, keepdims=True))
    grad_scores = rounded(probs * (grad_probs - delta) * scale)
    grad_q = jnp.einsum('hcs,shd->chd', grad_scores, key_heads).reshape(-1, width)
    grad_k = jnp.einsum('hcs,chd->shd', grad_scores, query_heads).reshape(-1, width)
    grad_mixed = jnp.concatenate([grad_q, grad_k, grad_vals], axis=-1).astype(jnp.bfloat16)
    g_qkv = jnp.dot(hidden_a.T, grad_mixed, preferred_element_type=jnp.float32)
    grad_ha = jnp.dot(grad_mixed, w_qkv.T, preferred_element_type=jnp.float32)
    grad_rows = grad_resid + norm_back(grad_ha, normed_a, inverse_a, gain[0])
    g_gains = jnp.stack([lax.optimization_barrier(jnp.sum(grad_ha * normed_a, axis=0)), lax.optimization_barrier(jnp.sum(grad_hb * normed_b, axis=0))])
    g_biases = jnp.concatenate([jnp.stack([lax.optimization_barrier(jnp.sum(grad_ha, axis=0)), lax.optimization_barrier(jnp.sum(grad_q, axis=0)), lax.optimization_barrier(jnp.sum(grad_vals, axis=0)), lax.optimization_barrier(jnp.sum(grad_resid, axis=0)), lax.optimization_barrier(jnp.sum(grad_hb, axis=0)), lax.optimization_barrier(jnp.sum(grad_y, axis=0))]), lax.optimization_barrier(jnp.sum(grad_pre, axis=0)).reshape(-1, width)], axis=0)
    return ((output, grad_rows.astype(jnp.bfloat16)), (g_qkv, g_outw, g_up, g_down, g_gains, g_biases))

def adamw(param, grad, first, second):
    first_new = 0.9 * first + 0.1 * grad
    second_new = 0.95 * second + 0.05 * grad * grad
    step_size = first_new / (1.0 - 0.9 ** STEP) / (jnp.sqrt(second_new / (1.0 - 0.95 ** STEP)) + 1e-08)
    return (param - 0.004 * (step_size + 0.05 * param), first_new, second_new)

def reference(images, cotangent, w_qkv, w_out, w_up, w_down, gains, biases, first_qkv, first_out, first_up, first_down, first_gains, first_biases, second_qkv, second_out, second_up, second_down, second_gains, second_biases):
    params = (w_qkv, w_out, w_up, w_down, gains, biases)
    firsts = (first_qkv, first_out, first_up, first_down, first_gains, first_biases)
    seconds = (second_qkv, second_out, second_up, second_down, second_gains, second_biases)
    kernels = tuple((param.astype(jnp.bfloat16) for param in params))
    live = jnp.arange(SEQ_PAD) < PATCH_TOK

    def per_image(carry, item):
        outputs, grads = layer_pass(item[0], item[1], kernels, live)
        return (tuple((total + grad for total, grad in zip(carry, grads))), outputs)
    start = tuple((jnp.zeros(param.shape, jnp.float32) for param in params))
    totals, (out_images, grad_images) = lax.scan(per_image, start, (images, cotangent))
    updated = [adamw(param, grad, first, second) for param, grad, first, second in zip(params, totals, firsts, seconds)]
    news = tuple((entry[0] for entry in updated))
    new_firsts = tuple((entry[1] for entry in updated))
    new_seconds = tuple((entry[2] for entry in updated))
    return (out_images, grad_images, totals[0], totals[1], totals[2], totals[3], totals[4], totals[5], news[0], news[1], news[2], news[3], news[4], news[5], new_firsts[0], new_firsts[1], new_firsts[2], new_firsts[3], new_firsts[4], new_firsts[5], new_seconds[0], new_seconds[1], new_seconds[2], new_seconds[3], new_seconds[4], new_seconds[5])
```

```python
import functools

import jax
import jax.numpy as jnp
from jax import lax
from jax.experimental import pallas as pl
from jax.experimental.pallas import tpu as pltpu
from jax.sharding import PartitionSpec as P

HEAD_DIM = 64
PATCH_TOK = 577
STEP = 5


def normalize(rows):
    center = rows - jnp.mean(rows, axis=-1, keepdims=True)
    inverse = lax.rsqrt(jnp.mean(center * center, axis=-1, keepdims=True) + 1e-06)
    return (center * inverse, inverse)


def norm_back(grad_out, normed, inverse, gain):
    scaled = grad_out * gain
    return inverse * (
        scaled
        - jnp.mean(scaled, axis=-1, keepdims=True)
        - normed * jnp.mean(scaled * normed, axis=-1, keepdims=True)
    )


def gelu_value(pre):
    return pre * 0.5 * (1.0 + lax.erf(pre * 0.7071067811865476))


def gelu_slope(pre):
    return (
        0.5 * (1.0 + lax.erf(pre * 0.7071067811865476))
        + pre * jnp.exp(-0.5 * pre * pre) * 0.3989422804014327
    )


def adamw(param, grad, first, second):
    first_new = 0.9 * first + 0.1 * grad
    second_new = 0.95 * second + 0.05 * grad * grad
    step_size = first_new / (1.0 - 0.9**STEP) / (jnp.sqrt(second_new / (1.0 - 0.95**STEP)) + 1e-08)
    return (param - 0.004 * (step_size + 0.05 * param), first_new, second_new)


LANES = 128
NT = (((1,), (1,)), ((), ()))
NN = (((1,), (0,)), ((), ()))
TN = (((0,), (0,)), ((), ()))


def dot(a, b, dims):
    return lax.dot_general(a, b, dims, preferred_element_type=jnp.float32)


def head_masks(rows, dtype):
    lane = lax.broadcasted_iota(jnp.int32, (rows, LANES), 1)
    return [
        ((lane >= h * HEAD_DIM) & (lane < (h + 1) * HEAD_DIM)) for h in range(LANES // HEAD_DIM)
    ]


def attend_kernel(q_ref, k_ref, v_ref, live_ref, ctx_ref):
    q, k, v = q_ref[0], k_ref[0], v_ref[0]
    live = live_ref[...] > 0.5
    total = jnp.zeros(q.shape, jnp.float32)
    zero = jnp.zeros_like(q)
    for mask in head_masks(q.shape[0], q.dtype):
        scores = dot(jnp.where(mask, q, zero), k, NT) * (HEAD_DIM**-0.5)
        scores = jnp.where(live, scores, -1e30)
        top = jnp.max(scores, axis=-1, keepdims=True)
        weights = jnp.exp(scores - top)
        denom = jnp.sum(weights, axis=-1, keepdims=True)
        probs = (weights * (1.0 / denom)).astype(jnp.bfloat16)
        total = jnp.where(mask, dot(probs, v, NN), total)
    ctx_ref[0] = total.astype(jnp.bfloat16)


def attend_back_kernel(q_ref, k_ref, v_ref, g_ref, live_ref, dq_ref, dk_ref, dv_ref):
    q, k, v, g = q_ref[0], k_ref[0], v_ref[0], g_ref[0]
    live = live_ref[...] > 0.5
    zero_q = jnp.zeros_like(q)
    zero_k = jnp.zeros_like(k)
    dq = jnp.zeros(q.shape, jnp.float32)
    dk = jnp.zeros(k.shape, jnp.float32)
    dv = jnp.zeros(k.shape, jnp.float32)
    masks_q = head_masks(q.shape[0], q.dtype)
    masks_k = head_masks(k.shape[0], k.dtype)
    for mask, mask_k in zip(masks_q, masks_k):
        q_h = jnp.where(mask, q, zero_q)
        g_h = jnp.where(mask, g, zero_q)
        k_h = jnp.where(mask_k, k, zero_k)
        scores = dot(k, q_h, NT) * (HEAD_DIM**-0.5)
        scores = jnp.where(live, scores, -1e30)
        top = jnp.max(scores, axis=0, keepdims=True)
        weights = jnp.exp(scores - top)
        denom = jnp.sum(weights, axis=0, keepdims=True)
        probs = weights * (1.0 / denom)
        grad_probs = dot(v, g_h, NT)
        delta = jnp.sum(probs * grad_probs, axis=0, keepdims=True)
        grad_scores = (probs * (grad_probs - delta) * (HEAD_DIM**-0.5)).astype(jnp.bfloat16)
        dv = dv + dot(probs.astype(jnp.bfloat16), g_h, NN)
        dk = dk + dot(grad_scores, q_h, NN)
        dq = dq + dot(grad_scores, k_h, TN)
    dq_ref[0] = dq
    dk_ref[0] = dk.astype(dk_ref.dtype)
    dv_ref[0] = dv.astype(dv_ref.dtype)


def attend(queries, keys, values, live):
    count, rows, width = queries.shape
    length = keys.shape[1]
    q_spec = pl.BlockSpec((1, rows, LANES), lambda i, h: (i, 0, h))
    k_spec = pl.BlockSpec((1, length, LANES), lambda i, h: (i, 0, h))
    pairs = count * rows * length * width
    return pl.pallas_call(
        attend_kernel,
        grid=(count, width // LANES),
        in_specs=[q_spec, k_spec, k_spec, pl.BlockSpec((1, length), lambda i, h: (0, 0))],
        out_specs=q_spec,
        out_shape=jax.ShapeDtypeStruct(queries.shape, jnp.bfloat16),
        cost_estimate=pl.CostEstimate(
            flops=8 * pairs, bytes_accessed=8 * queries.size, transcendentals=pairs // HEAD_DIM
        ),
        compiler_params=pltpu.CompilerParams(vmem_limit_bytes=48 * 1024 * 1024),
    )(queries, keys, values, live.reshape(1, length))


def attend_back(queries, keys, values, grad_ctx, live, back_dtype):
    count, rows, width = queries.shape
    length = keys.shape[1]
    q_spec = pl.BlockSpec((1, rows, LANES), lambda i, h: (i, 0, h))
    k_spec = pl.BlockSpec((1, length, LANES), lambda i, h: (i, 0, h))
    pairs = count * rows * length * width
    return pl.pallas_call(
        attend_back_kernel,
        grid=(count, width // LANES),
        in_specs=[q_spec, k_spec, k_spec, q_spec, pl.BlockSpec((length, 1), lambda i, h: (0, 0))],
        out_specs=[q_spec, k_spec, k_spec],
        out_shape=[
            jax.ShapeDtypeStruct(queries.shape, jnp.float32),
            jax.ShapeDtypeStruct(keys.shape, back_dtype),
            jax.ShapeDtypeStruct(keys.shape, back_dtype),
        ],
        cost_estimate=pl.CostEstimate(
            flops=20 * pairs, bytes_accessed=20 * queries.size, transcendentals=pairs // HEAD_DIM
        ),
        compiler_params=pltpu.CompilerParams(vmem_limit_bytes=56 * 1024 * 1024),
    )(queries, keys, values, grad_ctx, live.reshape(length, 1))


def shift_by(step, ways):
    return [(i, (i + step) % ways) for i in range(ways)]


def spread(tokens):
    ways = lax.axis_size("seq")
    me = lax.axis_index("seq")
    each = tokens.shape[0] // ways
    parts = [lax.dynamic_slice_in_dim(tokens, me * each, each, 0)]
    for step in range(1, ways):
        target = lax.rem(me + step, ways)
        piece = lax.dynamic_slice_in_dim(tokens, target * each, each, 0)
        parts.append(lax.ppermute(piece, "seq", shift_by(step, ways)))
    return jnp.concatenate(parts, axis=1)


def unspread(tokens):
    ways = lax.axis_size("seq")
    me = lax.axis_index("seq")
    each, length, width = tokens.shape
    group = length // ways
    result = jnp.zeros((each * ways, group, width), tokens.dtype)
    for step in range(ways):
        piece = tokens[:, step * group : (step + 1) * group]
        if step:
            piece = lax.ppermute(piece, "seq", shift_by(-step, ways))
        source = lax.rem(me + step, ways)
        result = lax.dynamic_update_slice_in_dim(result, piece, source * each, 0)
    return result


def sum_over_seq(terms, axis):
    ways = lax.axis_size("seq")
    me = lax.axis_index("seq")
    size = terms.shape[axis] // ways
    total = lax.dynamic_slice_in_dim(terms, me * size, size, axis).astype(jnp.float32)
    for step in range(1, ways):
        target = lax.rem(me + step, ways)
        piece = lax.dynamic_slice_in_dim(terms, target * size, size, axis)
        total = total + lax.ppermute(piece, "seq", shift_by(step, ways)).astype(jnp.float32)
    return total


MESH = pl.DeviceIdType.MESH


def place():
    d = lax.axis_index("dp")
    return lax.rem(d, 2), lax.rem(d // 2, 2), d // 4, lax.axis_index("seq")


def greet(core, x, z, y, depth):
    barrier = pltpu.get_barrier_semaphore()
    others = [site(core, x, lax.rem(z + k, depth), y) for k in range(1, depth)]
    others += [site(core, 1 - x, z, y), site(core, x, z, 1 - y), site(1 - core, x, z, y)]
    for other in others:
        pl.semaphore_signal(barrier, inc=1, device_id=other, device_id_type=MESH)
    pl.semaphore_wait(barrier, len(others))


def site(core, x, z, y):
    return {"dp": (z * 2 + x) * 2 + core, "seq": y}


def columns(index, size):
    return pl.ds(pl.multiple_of(index * size, LANES), size)


def gather_kernel(parts, depth, count, *refs):
    shards, outs = refs[:count], refs[count : 2 * count]
    own_sem, send, recv = refs[2 * count :]
    core, x, z, y = place()
    greet(core, x, z, y, depth)
    pending = []

    def push(src, dst, p, lane, target):
        copy = pltpu.make_async_remote_copy(
            src_ref=src,
            dst_ref=dst,
            send_sem=send.at[p, lane],
            recv_sem=recv.at[p, lane],
            device_id=target,
            device_id_type=MESH,
        )
        copy.start()
        pending.append(copy)
        return copy

    def view(p):
        w, start, size, kind = parts[p]
        return shards[w].at[start : start + size], outs[w], pl.ds(start, size), shards[w].shape[1], kind

    state = {}

    def stage0(p):
        src, out, rows, width, kind = view(p)
        mine = out.at[z, x, core, rows, columns(y, width)]
        local = pltpu.make_async_copy(src, mine, own_sem.at[p])
        local.start()
        state[p] = [local] + [
            push(src, mine, p, k - 1, site(core, x, lax.rem(z + k, depth), y))
            for k in range(1, depth)
        ]

    def stage1(p):
        src, out, rows, width, kind = view(p)
        state[p][0].wait()
        for copy in state[p][1:]:
            copy.wait_recv()
        block = out.at[:, x, core, rows, columns(y, width)]
        target = site(core, 1 - x, z, y) if kind == 0 else site(core, x, z, 1 - y)
        state[p] = push(block, block, p, depth - 1, target)

    def stage2(p):
        src, out, rows, width, kind = view(p)
        state[p].wait_recv()
        if kind == 0:
            block = out.at[:, :, core, rows, columns(y, width)]
            state[p] = push(block, block, p, depth, site(core, x, z, 1 - y))
        else:
            block = out.at[:, x, core, rows, :]
            state[p] = push(block, block, p, depth, site(core, 1 - x, z, y))

    def stage3(p):
        src, out, rows, width, kind = view(p)
        state[p].wait_recv()
        block = out.at[:, :, core, rows, :]
        state[p] = push(block, block, p, depth + 1, site(1 - core, x, z, y))

    def stage4(p):
        state[p].wait_recv()

    total = len(parts)
    for p in range(total):
        stage0(p)
    for step in range(total // 2 + 3):
        for lag, stage in enumerate((stage1, stage2, stage3, stage4)):
            for p in (2 * (step - lag), 2 * (step - lag) + 1):
                if 0 <= p < total:
                    stage(p)
    for copy in pending:
        copy.wait_send()


def split_rows(shapes, pieces):
    parts = []
    for w, (shape, n) in enumerate(zip(shapes, pieces)):
        size = shape[0] // n
        parts += [(w, i * size, size, i % 2) for i in range(n)]
    return parts


def gather(shards, pieces, cid, depth):
    parts = split_rows([s.shape for s in shards], pieces)
    total = len(parts)
    outs = pl.pallas_call(
        functools.partial(gather_kernel, parts, depth, len(shards)),
        in_specs=[pl.BlockSpec(memory_space=pltpu.VMEM)] * len(shards),
        out_specs=[pl.BlockSpec(memory_space=pl.ANY)] * len(shards),
        out_shape=[
            jax.ShapeDtypeStruct((depth, 2, 2, s.shape[0], 2 * s.shape[1]), s.dtype) for s in shards
        ],
        scratch_shapes=[
            pltpu.SemaphoreType.DMA((total,)),
            pltpu.SemaphoreType.DMA((total, depth + 2)),
            pltpu.SemaphoreType.DMA((total, depth + 2)),
        ],
        compiler_params=pltpu.CompilerParams(collective_id=cid, has_side_effects=True),
    )(*shards)
    return [o.reshape(-1, o.shape[-1]) for o in outs]


def reduce_kernel(parts, depth, count, shapes, *refs):
    grads, outs = refs[:count], refs[count : 2 * count]
    own, near = refs[2 * count : 3 * count], refs[3 * count : 4 * count]
    mid, side, far, last = (refs[i * count : (i + 1) * count] for i in (4, 5, 6, 7))
    own_sem, send, recv = refs[8 * count :]
    core, x, z, y = place()
    greet(core, x, z, y, depth)
    pending = []

    def push(src, dst, p, lane, target):
        copy = pltpu.make_async_remote_copy(
            src_ref=src,
            dst_ref=dst,
            send_sem=send.at[p, lane],
            recv_sem=recv.at[p, lane],
            device_id=target,
            device_id_type=MESH,
        )
        copy.start()
        pending.append(copy)
        return copy

    def view(p):
        w, start, size, kind = parts[p]
        return w, pl.ds(start, size), shapes[w][1], kind

    state = {}

    def add(left, right):
        return left[...].astype(jnp.float32) + right[...].astype(jnp.float32)

    def stage0(p):
        w, rows, width, kind = view(p)
        local = pltpu.make_async_copy(
            grads[w].at[:, :, core, rows], own[w].at[:, :, rows], own_sem.at[p]
        )
        local.start()
        copy = push(
            grads[w].at[:, :, 1 - core, rows],
            near[w].at[:, :, rows],
            p,
            depth - 1,
            site(1 - core, x, z, y),
        )
        state[p] = (local, copy)

    def stage1(p):
        w, rows, width, kind = view(p)
        local, copy = state[p]
        local.wait()
        copy.wait_recv()

        def body(i, carry):
            mine = own[w].at[i // 2, lax.rem(i, 2), rows]
            mine[...] = add(mine, near[w].at[i // 2, lax.rem(i, 2), rows]).astype(jnp.bfloat16)
            return carry

        lax.fori_loop(0, 2 * depth, body, 0)
        if kind == 0:
            state[p] = push(
                own[w].at[:, :, rows, columns(1 - y, width)],
                mid[w].at[:, :, rows],
                p,
                depth,
                site(core, x, z, 1 - y),
            )
        else:
            state[p] = push(
                own[w].at[:, 1 - x, rows],
                side[w].at[:, rows],
                p,
                depth,
                site(core, 1 - x, z, y),
            )

    def stage2(p):
        w, rows, width, kind = view(p)
        state[p].wait_recv()
        if kind == 0:

            def body(i, carry):
                mine = own[w].at[i // 2, lax.rem(i, 2), rows, columns(y, width)]
                mine[...] = add(mine, mid[w].at[i // 2, lax.rem(i, 2), rows]).astype(jnp.bfloat16)
                return carry

            lax.fori_loop(0, 2 * depth, body, 0)
            state[p] = push(
                own[w].at[:, 1 - x, rows, columns(y, width)],
                far[w].at[:, rows],
                p,
                depth + 1,
                site(core, 1 - x, z, y),
            )
        else:

            def body(i, carry):
                mine = own[w].at[i, x, rows]
                mine[...] = add(mine, side[w].at[i, rows]).astype(jnp.bfloat16)
                return carry

            lax.fori_loop(0, depth, body, 0)
            state[p] = push(
                own[w].at[:, x, rows, columns(1 - y, width)],
                far[w].at[:, rows],
                p,
                depth + 1,
                site(core, x, z, 1 - y),
            )

    def stage3(p):
        w, rows, width, kind = view(p)
        state[p].wait_recv()

        def body(i, carry):
            mine = own[w].at[i, x, rows, columns(y, width)]
            mine[...] = add(mine, far[w].at[i, rows]).astype(jnp.bfloat16)
            return carry

        lax.fori_loop(0, depth, body, 0)
        state[p] = [
            push(
                own[w].at[lax.rem(z + k, depth), x, rows, columns(y, width)],
                last[w].at[k - 1, rows],
                p,
                k - 1,
                site(core, x, lax.rem(z + k, depth), y),
            )
            for k in range(1, depth)
        ]

    def stage4(p):
        w, rows, width, kind = view(p)
        for copy in state[p]:
            copy.wait_recv()
        total = own[w][z, x, rows, columns(y, width)].astype(jnp.float32)
        for k in range(depth - 1):
            total = total + last[w][k, rows].astype(jnp.float32)
        outs[w][rows] = total

    total = len(parts)
    for p in range(total):
        stage0(p)
    for step in range(total // 2 + 4):
        for lag, stage in enumerate((stage1, stage2, stage3, stage4)):
            for p in (2 * (step - lag), 2 * (step - lag) + 1):
                if 0 <= p < total:
                    stage(p)
    for copy in pending:
        copy.wait_send()


def reduce_sum(grads, pieces, cid, depth):
    count = len(grads)
    shapes = [(g.shape[0] // (4 * depth), g.shape[1] // 2) for g in grads]
    parts = split_rows(shapes, pieces)
    total = len(parts)

    def each(form):
        return [pltpu.VMEM(form(r, c), jnp.bfloat16) for r, c in shapes]

    return pl.pallas_call(
        functools.partial(reduce_kernel, parts, depth, count, shapes),
        in_specs=[pl.BlockSpec(memory_space=pl.ANY)] * count,
        out_specs=[pl.BlockSpec(memory_space=pltpu.VMEM)] * count,
        out_shape=[jax.ShapeDtypeStruct(s, jnp.float32) for s in shapes],
        scratch_shapes=each(lambda r, c: (depth, 2, r, 2 * c))
        + each(lambda r, c: (depth, 2, r, 2 * c))
        + each(lambda r, c: (depth, 2, r, c))
        + each(lambda r, c: (depth, r, 2 * c))
        + each(lambda r, c: (depth, r, c))
        + each(lambda r, c: (depth - 1, r, c))
        + [
            pltpu.SemaphoreType.DMA((total,)),
            pltpu.SemaphoreType.DMA((total, depth + 2)),
            pltpu.SemaphoreType.DMA((total, depth + 2)),
        ],
        compiler_params=pltpu.CompilerParams(
            collective_id=cid, has_side_effects=True, vmem_limit_bytes=56 * 1024 * 1024
        ),
    )(*[g.reshape(depth, 2, 2, r, 2 * c) for g, (r, c) in zip(grads, shapes)])


def general_body(
    images,
    cotangent,
    w_qkv,
    w_out,
    w_up,
    w_down,
    gains,
    biases,
    first_qkv,
    first_out,
    first_up,
    first_down,
    first_gains,
    first_biases,
    second_qkv,
    second_out,
    second_up,
    second_down,
    second_gains,
    second_biases,
):
    params = (w_qkv, w_out, w_up, w_down, gains, biases)
    firsts = (first_qkv, first_out, first_up, first_down, first_gains, first_biases)
    seconds = (second_qkv, second_out, second_up, second_down, second_gains, second_biases)
    count, group, width = images.shape
    ways = lax.axis_size("seq")
    blocks = lax.axis_size("dp")
    me = lax.axis_index("seq")
    pad_len = group * ways
    by_image = count % ways == 0
    rows_dp = w_qkv.shape[0]
    cols = w_out.shape[1]
    fold = w_up.shape[1] // cols
    own = gains.shape[1]
    small = jnp.concatenate([gains, biases], axis=0).astype(jnp.bfloat16).T
    lanes = -(-small.shape[1] // LANES) * LANES
    small = jnp.pad(small, ((0, rows_dp - own), (0, lanes - small.shape[1])))
    part_a = jnp.concatenate([w_qkv.astype(jnp.bfloat16), small], axis=1)
    wide_a = lax.all_gather(part_a, ("seq", "dp"), axis=0, tiled=True)
    part_b = jnp.concatenate(
        [
            w_out.astype(jnp.bfloat16),
            w_up.astype(jnp.bfloat16)
            .reshape(rows_dp, fold, cols)
            .transpose(1, 0, 2)
            .reshape(fold * rows_dp, cols),
            w_down.astype(jnp.bfloat16),
        ],
        axis=0,
    )
    part_b, wide_a = lax.optimization_barrier((part_b, wide_a))
    wide_b = lax.all_gather(part_b, ("seq", "dp"), axis=0, tiled=True)
    wide_a = wide_a.reshape(ways, width, part_a.shape[1])
    wide_qkv = jnp.concatenate([wide_a[k, :, : w_qkv.shape[1]] for k in range(ways)], axis=1)
    wide_small = (
        wide_a.reshape(ways, blocks, rows_dp, part_a.shape[1])[
            :, :, :own, w_qkv.shape[1] : w_qkv.shape[1] + 12
        ]
        .astype(jnp.float32)
        .transpose(3, 1, 0, 2)
        .reshape(12, width)
    )
    gain, bias = wide_small[:2], wide_small[2:]
    back_gain = gain
    wide_b = wide_b.reshape(ways, blocks, part_b.shape[0], cols)
    wide_out = wide_b[:, :, :rows_dp].transpose(1, 2, 0, 3).reshape(width, width)
    wide_up = (
        wide_b[:, :, rows_dp : (1 + fold) * rows_dp]
        .reshape(ways, blocks, fold, rows_dp, cols)
        .transpose(1, 3, 0, 2, 4)
        .reshape(width, fold * width)
    )
    wide_down = (
        wide_b[:, :, (1 + fold) * rows_dp :].transpose(1, 2, 0, 3).reshape(fold * width, width)
    )
    back_qkv, back_out, back_up, back_down = wide_qkv, wide_out, wide_up, wide_down
    spot = jnp.arange(group, dtype=jnp.int32)
    if by_image:
        images, cotangent = spread(images), spread(cotangent)
        token_live = jnp.concatenate(
            [lax.rem(me - k + ways, ways) * group + spot for k in range(ways)]
        ) < PATCH_TOK
        key_live = token_live
    else:
        token_live = me * group + spot < PATCH_TOK
        key_live = jnp.arange(pad_len, dtype=jnp.int32) < PATCH_TOK
    query_live = token_live
    key_live = key_live.astype(jnp.float32)
    rows = images.astype(jnp.float32)
    normed_a, inverse_a = normalize(rows)
    hidden_a = (normed_a * gain[0] + bias[0]).astype(jnp.bfloat16)
    mixed = jnp.einsum("icd,de->ice", hidden_a, wide_qkv, preferred_element_type=jnp.float32)
    queries = (mixed[..., :width] + bias[1]).astype(jnp.bfloat16)
    keys = mixed[..., width : 2 * width].astype(jnp.bfloat16)
    values = (mixed[..., 2 * width :] + bias[2]).astype(jnp.bfloat16)
    if by_image:
        keys_all, values_all = keys, values
    else:
        keys_all, values_all = (
            lax.all_gather(keys, "seq", axis=1, tiled=True),
            lax.all_gather(values, "seq", axis=1, tiled=True),
        )
    context = attend(queries, keys_all, values_all, key_live)
    resid = (
        rows
        + jnp.einsum("icd,de->ice", context, wide_out, preferred_element_type=jnp.float32)
        + bias[3]
    )
    normed_b, inverse_b = normalize(resid)
    hidden_b = (normed_b * gain[1] + bias[4]).astype(jnp.bfloat16)
    pre = jnp.einsum("icd,df->icf", hidden_b, wide_up, preferred_element_type=jnp.float32) + bias[
        6:
    ].reshape(-1)
    active = gelu_value(pre).astype(jnp.bfloat16)
    out_images = (
        resid
        + jnp.einsum("icf,fd->icd", active, wide_down, preferred_element_type=jnp.float32)
        + bias[5]
    ).astype(jnp.bfloat16)
    grad_y = cotangent.astype(jnp.float32) * query_live[None, :, None].astype(jnp.float32)
    grad_yb = grad_y.astype(jnp.bfloat16)
    g_down = jnp.einsum("icf,icd->fd", active, grad_yb, preferred_element_type=jnp.float32)
    grad_pre = jnp.einsum(
        "icd,fd->icf", grad_yb, back_down, preferred_element_type=jnp.float32
    ) * gelu_slope(pre)
    grad_preb = grad_pre.astype(jnp.bfloat16)
    g_up = jnp.einsum("icd,icf->df", hidden_b, grad_preb, preferred_element_type=jnp.float32)
    grad_hb = jnp.einsum("icf,df->icd", grad_preb, back_up, preferred_element_type=jnp.float32)
    grad_resid = grad_y + norm_back(grad_hb, normed_b, inverse_b, back_gain[1])
    grad_rb = grad_resid.astype(jnp.bfloat16)
    g_outw = jnp.einsum("icd,ice->de", context, grad_rb, preferred_element_type=jnp.float32)
    grad_ctx = jnp.einsum(
        "ice,de->icd", grad_rb, back_out, preferred_element_type=jnp.float32
    ).astype(jnp.bfloat16)
    grad_q, grad_k, grad_v = attend_back(
        queries,
        keys_all,
        values_all,
        grad_ctx,
        key_live,
        jnp.float32 if by_image else jnp.bfloat16,
    )
    if not by_image:
        grad_k, grad_v = (
            lax.psum_scatter(grad_k, "seq", scatter_dimension=1, tiled=True).astype(jnp.float32),
            lax.psum_scatter(grad_v, "seq", scatter_dimension=1, tiled=True).astype(jnp.float32),
        )
    grad_mixed = jnp.concatenate([grad_q, grad_k, grad_v], axis=-1).astype(jnp.bfloat16)
    g_qkv = jnp.einsum("icd,ice->de", hidden_a, grad_mixed, preferred_element_type=jnp.float32)
    grad_ha = jnp.einsum("ice,de->icd", grad_mixed, back_qkv, preferred_element_type=jnp.float32)
    grad_images = (grad_resid + norm_back(grad_ha, normed_a, inverse_a, back_gain[0])).astype(
        jnp.bfloat16
    )
    g_gains = jnp.stack(
        [jnp.sum(grad_ha * normed_a, axis=(0, 1)), jnp.sum(grad_hb * normed_b, axis=(0, 1))]
    )
    g_biases = jnp.concatenate(
        [
            jnp.stack(
                [
                    jnp.sum(grad_ha, axis=(0, 1)),
                    jnp.sum(grad_q, axis=(0, 1)),
                    jnp.sum(grad_v, axis=(0, 1)),
                    jnp.sum(grad_resid, axis=(0, 1)),
                    jnp.sum(grad_hb, axis=(0, 1)),
                    jnp.sum(grad_y, axis=(0, 1)),
                ]
            ),
            jnp.sum(grad_pre, axis=(0, 1)).reshape(-1, width),
        ],
        axis=0,
    )
    if by_image:
        out_images, grad_images = unspread(out_images), unspread(grad_images)
    send_a = jnp.concatenate(
        [
            g_outw.astype(jnp.bfloat16).reshape(blocks, rows_dp, width),
            g_up.astype(jnp.bfloat16)
            .reshape(blocks, rows_dp, ways, fold, cols)
            .transpose(0, 3, 1, 2, 4)
            .reshape(blocks, fold * rows_dp, width),
            g_down.astype(jnp.bfloat16).reshape(blocks, fold * rows_dp, width),
        ],
        axis=1,
    ).reshape(-1, width)
    part = lax.psum_scatter(send_a, "dp", scatter_dimension=0, tiled=True)
    total_a = sum_over_seq(part, 1)
    g_small = jnp.concatenate([g_gains, g_biases], axis=0).astype(jnp.bfloat16).T
    g_small = jnp.pad(g_small, ((0, 0), (0, lanes - g_small.shape[1])))
    send_b = jnp.concatenate([g_qkv.astype(jnp.bfloat16), g_small], axis=1)
    part, _ = lax.optimization_barrier((send_b, part))
    part = lax.psum_scatter(part, "dp", scatter_dimension=0, tiled=True)
    total_qkv = sum_over_seq(part[:, : g_qkv.shape[1]], 1)
    total_small = sum_over_seq(part[:, g_qkv.shape[1] :], 0)[:, :12].T
    totals = (
        total_qkv,
        total_a[:rows_dp],
        total_a[rows_dp : (1 + fold) * rows_dp]
        .reshape(fold, rows_dp, cols)
        .transpose(1, 0, 2)
        .reshape(rows_dp, fold * cols),
        total_a[(1 + fold) * rows_dp :],
        total_small[:2],
        total_small[2:],
    )
    updated = [
        adamw(param, grad, first, second)
        for param, grad, first, second in zip(params, totals, firsts, seconds)
    ]
    news = tuple((entry[0] for entry in updated))
    new_firsts = tuple((entry[1] for entry in updated))
    new_seconds = tuple((entry[2] for entry in updated))
    return (
        out_images,
        grad_images,
        totals[0],
        totals[1],
        totals[2],
        totals[3],
        totals[4],
        totals[5],
        news[0],
        news[1],
        news[2],
        news[3],
        news[4],
        news[5],
        new_firsts[0],
        new_firsts[1],
        new_firsts[2],
        new_firsts[3],
        new_firsts[4],
        new_firsts[5],
        new_seconds[0],
        new_seconds[1],
        new_seconds[2],
        new_seconds[3],
        new_seconds[4],
        new_seconds[5],
    )


def is_paired(mesh):
    return mesh.shape["seq"] == 2 and mesh.shape["dp"] % 4 == 0


def attend_mixed_kernel(q_ref, k_ref, v_ref, live_ref, ctx_ref):
    attend_kernel(q_ref, k_ref, v_ref, live_ref, ctx_ref)


def attend_mixed(mixed, live):
    count, rows, triple = mixed.shape
    width = triple // 3
    heads = width // LANES
    specs = [
        pl.BlockSpec((1, rows, LANES), lambda i, h, k=k: (i, 0, h + k * heads)) for k in range(3)
    ]
    pairs = count * rows * rows * width
    return pl.pallas_call(
        attend_mixed_kernel,
        grid=(count, heads),
        in_specs=specs + [pl.BlockSpec((1, rows), lambda i, h: (0, 0))],
        out_specs=specs[0],
        out_shape=jax.ShapeDtypeStruct((count, rows, width), jnp.bfloat16),
        cost_estimate=pl.CostEstimate(
            flops=8 * pairs, bytes_accessed=2 * mixed.size, transcendentals=pairs // HEAD_DIM
        ),
        compiler_params=pltpu.CompilerParams(vmem_limit_bytes=48 * 1024 * 1024),
    )(mixed, mixed, mixed, live.reshape(1, rows))


def attend_back_mixed_kernel(q_ref, k_ref, v_ref, g_ref, live_ref, dm_ref, sum_ref, dq, dk, dv):
    attend_back_kernel(q_ref, k_ref, v_ref, g_ref, live_ref, dq, dk, dv)
    image, head = pl.program_id(0), pl.program_id(1)
    width = dm_ref.shape[2] // 3

    @pl.when(jnp.logical_and(image == 0, head == 0))
    def _():
        sum_ref[...] = jnp.zeros_like(sum_ref)

    for k, part in enumerate((dq, dk, dv)):
        where = pl.ds(pl.multiple_of(k * width + head * LANES, LANES), LANES)
        dm_ref[0, :, where] = part[0].astype(jnp.bfloat16)
        sum_ref[:, where] += jnp.sum(part[0], axis=0, keepdims=True)


def attend_back_mixed(mixed, grad_ctx, live):
    count, rows, triple = mixed.shape
    width = triple // 3
    heads = width // LANES
    specs = [
        pl.BlockSpec((1, rows, LANES), lambda i, h, k=k: (i, 0, h + k * heads)) for k in range(3)
    ]
    pairs = count * rows * rows * width
    return pl.pallas_call(
        attend_back_mixed_kernel,
        grid=(count, heads),
        in_specs=specs + [specs[0], pl.BlockSpec((rows, 1), lambda i, h: (0, 0))],
        out_specs=[
            pl.BlockSpec((1, rows, triple), lambda i, h: (i, 0, 0)),
            pl.BlockSpec((1, triple), lambda i, h: (0, 0)),
        ],
        out_shape=[
            jax.ShapeDtypeStruct(mixed.shape, jnp.bfloat16),
            jax.ShapeDtypeStruct((1, triple), jnp.float32),
        ],
        scratch_shapes=[pltpu.VMEM((1, rows, LANES), jnp.float32)] * 3,
        cost_estimate=pl.CostEstimate(
            flops=20 * pairs, bytes_accessed=4 * mixed.size, transcendentals=pairs // HEAD_DIM
        ),
        compiler_params=pltpu.CompilerParams(vmem_limit_bytes=56 * 1024 * 1024),
    )(mixed, mixed, mixed, grad_ctx, live.reshape(rows, 1))


def product(a, b, dims=NN):
    return lax.dot_general(a, b, dims, preferred_element_type=jnp.float32)


def fast_body(images, cotangent, *rest):
    params, firsts, seconds = rest[:6], rest[6:12], rest[12:]
    w_qkv, w_out, w_up, w_down, gains, biases = params
    count, group, width = images.shape
    ways = lax.axis_size("seq")
    blocks = lax.axis_size("dp")
    depth = blocks // 4
    me = lax.axis_index("seq")
    narrow = jnp.bfloat16
    vectors = gains.shape[0] + biases.shape[0]
    own = gains.shape[1]
    lanes = -(-own // LANES) * LANES
    tall = -(-vectors // 32) * 32
    small = jnp.concatenate([gains, biases], axis=0).astype(narrow)
    small = jnp.pad(small, ((0, tall - vectors), (0, lanes - own)))
    images, cotangent = spread(images), spread(cotangent)
    each, length = images.shape[:2]
    wide_qkv, wide_small, wide_out, wide_up, wide_down = gather(
        [w_qkv.astype(narrow), small, w_out.astype(narrow), w_up.astype(narrow), w_down.astype(narrow)],
        (4, 2, 2, 4, 4),
        1,
        depth,
    )
    wide_small = (
        wide_small.reshape(blocks, tall, ways, lanes)[:, :vectors, :, :own]
        .astype(jnp.float32)
        .transpose(1, 0, 2, 3)
        .reshape(vectors, width)
    )
    gain, bias = wide_small[: gains.shape[0]], wide_small[gains.shape[0] :]
    spot = jnp.arange(group, dtype=jnp.int32)
    live = jnp.concatenate(
        [lax.rem(me - k + ways, ways) * group + spot for k in range(ways)]
    ) < PATCH_TOK
    key_live = live.astype(jnp.float32)
    rows = images.reshape(each * length, width).astype(jnp.float32)
    normed_a, inverse_a = normalize(rows)
    hidden_a = (normed_a * gain[0] + bias[0]).astype(narrow)
    shift = jnp.concatenate([bias[1], jnp.zeros_like(bias[1]), bias[2]])
    mixed = (product(hidden_a, wide_qkv) + shift).astype(narrow).reshape(each, length, 3 * width)
    context = attend_mixed(mixed, key_live).reshape(each * length, width)
    resid = rows + product(context, wide_out) + bias[3]
    normed_b, inverse_b = normalize(resid)
    hidden_b = (normed_b * gain[1] + bias[4]).astype(narrow)
    pre = product(hidden_b, wide_up) + bias[6:].reshape(-1)
    active = gelu_value(pre).astype(narrow)
    out_images = (resid + product(active, wide_down) + bias[5]).astype(narrow)
    out_images = unspread(out_images.reshape(each, length, width))
    grad_y = cotangent.astype(jnp.float32) * live[None, :, None].astype(jnp.float32)
    grad_y = grad_y.reshape(each * length, width)
    grad_yb = grad_y.astype(narrow)
    g_down = product(active, grad_yb, TN)
    grad_pre = product(grad_yb, wide_down, NT) * gelu_slope(pre)
    grad_preb = grad_pre.astype(narrow)
    g_up = product(hidden_b, grad_preb, TN)
    grad_hb = product(grad_preb, wide_up, NT)
    grad_resid = grad_y + norm_back(grad_hb, normed_b, inverse_b, gain[1])
    grad_rb = grad_resid.astype(narrow)
    g_outw = product(context, grad_rb, TN)
    grad_ctx = product(grad_rb, wide_out, NT).astype(narrow).reshape(each, length, width)
    grad_mixed, mixed_sum = attend_back_mixed(mixed, grad_ctx, key_live)
    grad_mixed = grad_mixed.reshape(each * length, 3 * width)
    g_qkv = product(hidden_a, grad_mixed, TN)
    grad_ha = product(grad_mixed, wide_qkv, NT)
    grad_images = (grad_resid + norm_back(grad_ha, normed_a, inverse_a, gain[0])).astype(narrow)
    grad_images = unspread(grad_images.reshape(each, length, width))
    g_small = jnp.concatenate(
        [
            jnp.stack(
                [
                    jnp.sum(grad_ha * normed_a, axis=0),
                    jnp.sum(grad_hb * normed_b, axis=0),
                    jnp.sum(grad_ha, axis=0),
                    mixed_sum[0, :width],
                    mixed_sum[0, 2 * width :],
                    jnp.sum(grad_resid, axis=0),
                    jnp.sum(grad_hb, axis=0),
                    jnp.sum(grad_y, axis=0),
                ]
            ),
            jnp.sum(grad_pre, axis=0).reshape(-1, width),
        ],
        axis=0,
    )
    g_small = g_small.reshape(vectors, blocks, ways, own).transpose(1, 0, 2, 3)
    g_small = jnp.pad(g_small, ((0, 0), (0, tall - vectors), (0, 0), (0, lanes - own)))
    g_small = g_small.reshape(blocks * tall, ways * lanes)
    t_down, t_up, t_out, t_qkv, t_small = reduce_sum(
        [g.astype(narrow) for g in (g_down, g_up, g_outw, g_qkv, g_small)],
        (4, 4, 2, 4, 2),
        2,
        depth,
    )
    t_small = t_small[:vectors, :own]
    totals = (t_qkv, t_out, t_up, t_down, t_small[: gains.shape[0]], t_small[gains.shape[0] :])
    updated = [
        adamw(param, grad, first, second)
        for param, grad, first, second in zip(params, totals, firsts, seconds)
    ]
    return (
        out_images,
        grad_images,
        *totals,
        *(entry[0] for entry in updated),
        *(entry[1] for entry in updated),
        *(entry[2] for entry in updated),
    )


def solution(mesh):
    body = fast_body if is_paired(mesh) else general_body
    return jax.shard_map(
        body,
        mesh=mesh,
        in_specs=(
            P("dp", "seq", None),
            P("dp", "seq", None),
            P("dp", "seq"),
            P("dp", "seq"),
            P("dp", "seq"),
            P("dp", "seq"),
            P(None, ("dp", "seq")),
            P(None, ("dp", "seq")),
            P("dp", "seq"),
            P("dp", "seq"),
            P("dp", "seq"),
            P("dp", "seq"),
            P(None, ("dp", "seq")),
            P(None, ("dp", "seq")),
            P("dp", "seq"),
            P("dp", "seq"),
            P("dp", "seq"),
            P("dp", "seq"),
            P(None, ("dp", "seq")),
            P(None, ("dp", "seq")),
        ),
        out_specs=(
            P("dp", "seq", None),
            P("dp", "seq", None),
            P("dp", "seq"),
            P("dp", "seq"),
            P("dp", "seq"),
            P("dp", "seq"),
            P(None, ("dp", "seq")),
            P(None, ("dp", "seq")),
            P("dp", "seq"),
            P("dp", "seq"),
            P("dp", "seq"),
            P("dp", "seq"),
            P(None, ("dp", "seq")),
            P(None, ("dp", "seq")),
            P("dp", "seq"),
            P("dp", "seq"),
            P("dp", "seq"),
            P("dp", "seq"),
            P(None, ("dp", "seq")),
            P(None, ("dp", "seq")),
            P("dp", "seq"),
            P("dp", "seq"),
            P("dp", "seq"),
            P("dp", "seq"),
            P(None, ("dp", "seq")),
            P(None, ("dp", "seq")),
        ),
        check_vma=False,
    )
```

```python
import functools

import jax
import jax.numpy as jnp
from jax import lax
from jax.experimental import pallas as pl
from jax.experimental.pallas import tpu as pltpu
from jax.sharding import PartitionSpec as P

HEAD_DIM = 64
PATCH_TOK = 577
STEP = 5


def normalize(rows):
    center = rows - jnp.mean(rows, axis=-1, keepdims=True)
    inverse = lax.rsqrt(jnp.mean(center * center, axis=-1, keepdims=True) + 1e-06)
    return (center * inverse, inverse)


def norm_back(grad_out, normed, inverse, gain):
    scaled = grad_out * gain
    return inverse * (
        scaled
        - jnp.mean(scaled, axis=-1, keepdims=True)
        - normed * jnp.mean(scaled * normed, axis=-1, keepdims=True)
    )


def gelu_value(pre):
    return pre * 0.5 * (1.0 + lax.erf(pre * 0.7071067811865476))


def gelu_slope(pre):
    return (
        0.5 * (1.0 + lax.erf(pre * 0.7071067811865476))
        + pre * jnp.exp(-0.5 * pre * pre) * 0.3989422804014327
    )


def adamw(param, grad, first, second):
    first_new = 0.9 * first + 0.1 * grad
    second_new = 0.95 * second + 0.05 * grad * grad
    step_size = first_new / (1.0 - 0.9**STEP) / (jnp.sqrt(second_new / (1.0 - 0.95**STEP)) + 1e-08)
    return (param - 0.004 * (step_size + 0.05 * param), first_new, second_new)


LANES = 128
NT = (((1,), (1,)), ((), ()))
NN = (((1,), (0,)), ((), ()))
TN = (((0,), (0,)), ((), ()))


def dot(a, b, dims):
    return lax.dot_general(a, b, dims, preferred_element_type=jnp.float32)


def head_masks(rows, dtype):
    lane = lax.broadcasted_iota(jnp.int32, (rows, LANES), 1)
    return [
        ((lane >= h * HEAD_DIM) & (lane < (h + 1) * HEAD_DIM)) for h in range(LANES // HEAD_DIM)
    ]


def attend_kernel(q_ref, k_ref, v_ref, live_ref, ctx_ref):
    q, k, v = q_ref[0], k_ref[0], v_ref[0]
    live = live_ref[...] > 0.5
    total = jnp.zeros(q.shape, jnp.float32)
    zero = jnp.zeros_like(q)
    for mask in head_masks(q.shape[0], q.dtype):
        scores = dot(jnp.where(mask, q, zero), k, NT) * (HEAD_DIM**-0.5)
        scores = jnp.where(live, scores, -1e30)
        top = jnp.max(scores, axis=-1, keepdims=True)
        weights = jnp.exp(scores - top)
        denom = jnp.sum(weights, axis=-1, keepdims=True)
        probs = (weights * (1.0 / denom)).astype(jnp.bfloat16)
        total = jnp.where(mask, dot(probs, v, NN), total)
    ctx_ref[0] = total.astype(jnp.bfloat16)


def attend_back_kernel(q_ref, k_ref, v_ref, g_ref, live_ref, dq_ref, dk_ref, dv_ref):
    q, k, v, g = q_ref[0], k_ref[0], v_ref[0], g_ref[0]
    live = live_ref[...] > 0.5
    zero_q = jnp.zeros_like(q)
    zero_k = jnp.zeros_like(k)
    dq = jnp.zeros(q.shape, jnp.float32)
    dk = jnp.zeros(k.shape, jnp.float32)
    dv = jnp.zeros(k.shape, jnp.float32)
    masks_q = head_masks(q.shape[0], q.dtype)
    masks_k = head_masks(k.shape[0], k.dtype)
    for mask, mask_k in zip(masks_q, masks_k):
        q_h = jnp.where(mask, q, zero_q)
        g_h = jnp.where(mask, g, zero_q)
        k_h = jnp.where(mask_k, k, zero_k)
        scores = dot(k, q_h, NT) * (HEAD_DIM**-0.5)
        scores = jnp.where(live, scores, -1e30)
        top = jnp.max(scores, axis=0, keepdims=True)
        weights = jnp.exp(scores - top)
        denom = jnp.sum(weights, axis=0, keepdims=True)
        probs = weights * (1.0 / denom)
        grad_probs = dot(v, g_h, NT)
        delta = jnp.sum(probs * grad_probs, axis=0, keepdims=True)
        grad_scores = (probs * (grad_probs - delta) * (HEAD_DIM**-0.5)).astype(jnp.bfloat16)
        dv = dv + dot(probs.astype(jnp.bfloat16), g_h, NN)
        dk = dk + dot(grad_scores, q_h, NN)
        dq = dq + dot(grad_scores, k_h, TN)
    dq_ref[0] = dq
    dk_ref[0] = dk.astype(dk_ref.dtype)
    dv_ref[0] = dv.astype(dv_ref.dtype)


def attend(queries, keys, values, live):
    count, rows, width = queries.shape
    length = keys.shape[1]
    q_spec = pl.BlockSpec((1, rows, LANES), lambda i, h: (i, 0, h))
    k_spec = pl.BlockSpec((1, length, LANES), lambda i, h: (i, 0, h))
    pairs = count * rows * length * width
    return pl.pallas_call(
        attend_kernel,
        grid=(count, width // LANES),
        in_specs=[q_spec, k_spec, k_spec, pl.BlockSpec((1, length), lambda i, h: (0, 0))],
        out_specs=q_spec,
        out_shape=jax.ShapeDtypeStruct(queries.shape, jnp.bfloat16),
        cost_estimate=pl.CostEstimate(
            flops=8 * pairs, bytes_accessed=8 * queries.size, transcendentals=pairs // HEAD_DIM
        ),
        compiler_params=pltpu.CompilerParams(vmem_limit_bytes=48 * 1024 * 1024),
    )(queries, keys, values, live.reshape(1, length))


def attend_back(queries, keys, values, grad_ctx, live, back_dtype):
    count, rows, width = queries.shape
    length = keys.shape[1]
    q_spec = pl.BlockSpec((1, rows, LANES), lambda i, h: (i, 0, h))
    k_spec = pl.BlockSpec((1, length, LANES), lambda i, h: (i, 0, h))
    pairs = count * rows * length * width
    return pl.pallas_call(
        attend_back_kernel,
        grid=(count, width // LANES),
        in_specs=[q_spec, k_spec, k_spec, q_spec, pl.BlockSpec((length, 1), lambda i, h: (0, 0))],
        out_specs=[q_spec, k_spec, k_spec],
        out_shape=[
            jax.ShapeDtypeStruct(queries.shape, jnp.float32),
            jax.ShapeDtypeStruct(keys.shape, back_dtype),
            jax.ShapeDtypeStruct(keys.shape, back_dtype),
        ],
        cost_estimate=pl.CostEstimate(
            flops=20 * pairs, bytes_accessed=20 * queries.size, transcendentals=pairs // HEAD_DIM
        ),
        compiler_params=pltpu.CompilerParams(vmem_limit_bytes=56 * 1024 * 1024),
    )(queries, keys, values, grad_ctx, live.reshape(length, 1))


def shift_by(step, ways):
    return [(i, (i + step) % ways) for i in range(ways)]


def spread(tokens):
    ways = lax.axis_size("seq")
    me = lax.axis_index("seq")
    each = tokens.shape[0] // ways
    parts = [lax.dynamic_slice_in_dim(tokens, me * each, each, 0)]
    for step in range(1, ways):
        target = lax.rem(me + step, ways)
        piece = lax.dynamic_slice_in_dim(tokens, target * each, each, 0)
        parts.append(lax.ppermute(piece, "seq", shift_by(step, ways)))
    return jnp.concatenate(parts, axis=1)


def unspread(tokens):
    ways = lax.axis_size("seq")
    me = lax.axis_index("seq")
    each, length, width = tokens.shape
    group = length // ways
    result = jnp.zeros((each * ways, group, width), tokens.dtype)
    for step in range(ways):
        piece = tokens[:, step * group : (step + 1) * group]
        if step:
            piece = lax.ppermute(piece, "seq", shift_by(-step, ways))
        source = lax.rem(me + step, ways)
        result = lax.dynamic_update_slice_in_dim(result, piece, source * each, 0)
    return result


def sum_over_seq(terms, axis):
    ways = lax.axis_size("seq")
    me = lax.axis_index("seq")
    size = terms.shape[axis] // ways
    total = lax.dynamic_slice_in_dim(terms, me * size, size, axis).astype(jnp.float32)
    for step in range(1, ways):
        target = lax.rem(me + step, ways)
        piece = lax.dynamic_slice_in_dim(terms, target * size, size, axis)
        total = total + lax.ppermute(piece, "seq", shift_by(step, ways)).astype(jnp.float32)
    return total


MESH = pl.DeviceIdType.MESH


def place():
    d = lax.axis_index("dp")
    return lax.rem(d, 2), lax.rem(d // 2, 2), d // 4, lax.axis_index("seq")


def greet(core, x, z, y, depth):
    barrier = pltpu.get_barrier_semaphore()
    others = [site(core, x, lax.rem(z + k, depth), y) for k in range(1, depth)]
    others += [site(core, 1 - x, z, y), site(core, x, z, 1 - y), site(1 - core, x, z, y)]
    for other in others:
        pl.semaphore_signal(barrier, inc=1, device_id=other, device_id_type=MESH)
    pl.semaphore_wait(barrier, len(others))


def site(core, x, z, y):
    return {"dp": (z * 2 + x) * 2 + core, "seq": y}


def columns(index, size):
    return pl.ds(pl.multiple_of(index * size, LANES), size)


def gather_kernel(parts, depth, count, *refs):
    shards, outs = refs[:count], refs[count : 2 * count]
    own_sem, send, recv = refs[2 * count :]
    core, x, z, y = place()
    greet(core, x, z, y, depth)
    pending = []

    def push(src, dst, p, lane, target):
        copy = pltpu.make_async_remote_copy(
            src_ref=src,
            dst_ref=dst,
            send_sem=send.at[p, lane],
            recv_sem=recv.at[p, lane],
            device_id=target,
            device_id_type=MESH,
        )
        copy.start()
        pending.append(copy)
        return copy

    def view(p):
        w, start, size, kind = parts[p]
        return shards[w].at[start : start + size], outs[w], pl.ds(start, size), shards[w].shape[1], kind

    state = {}

    def stage0(p):
        src, out, rows, width, kind = view(p)
        mine = out.at[z, x, core, rows, columns(y, width)]
        local = pltpu.make_async_copy(src, mine, own_sem.at[p])
        local.start()
        state[p] = [local] + [
            push(src, mine, p, k - 1, site(core, x, lax.rem(z + k, depth), y))
            for k in range(1, depth)
        ]

    def stage1(p):
        src, out, rows, width, kind = view(p)
        state[p][0].wait()
        for copy in state[p][1:]:
            copy.wait_recv()
        block = out.at[:, x, core, rows, columns(y, width)]
        target = site(core, 1 - x, z, y) if kind == 0 else site(core, x, z, 1 - y)
        state[p] = push(block, block, p, depth - 1, target)

    def stage2(p):
        src, out, rows, width, kind = view(p)
        state[p].wait_recv()
        if kind == 0:
            block = out.at[:, :, core, rows, columns(y, width)]
            state[p] = push(block, block, p, depth, site(core, x, z, 1 - y))
        else:
            block = out.at[:, x, core, rows, :]
            state[p] = push(block, block, p, depth, site(core, 1 - x, z, y))

    def stage3(p):
        src, out, rows, width, kind = view(p)
        state[p].wait_recv()
        block = out.at[:, :, core, rows, :]
        state[p] = push(block, block, p, depth + 1, site(1 - core, x, z, y))

    def stage4(p):
        state[p].wait_recv()

    total = len(parts)
    for p in range(total):
        stage0(p)
    for step in range(total // 2 + 3):
        for lag, stage in enumerate((stage1, stage2, stage3, stage4)):
            for p in (2 * (step - lag), 2 * (step - lag) + 1):
                if 0 <= p < total:
                    stage(p)
    for copy in pending:
        copy.wait_send()


def split_rows(shapes, pieces):
    parts = []
    for w, (shape, n) in enumerate(zip(shapes, pieces)):
        size = shape[0] // n
        parts += [(w, i * size, size, i % 2) for i in range(n)]
    return parts


def gather(shards, pieces, cid, depth):
    parts = split_rows([s.shape for s in shards], pieces)
    total = len(parts)
    outs = pl.pallas_call(
        functools.partial(gather_kernel, parts, depth, len(shards)),
        in_specs=[pl.BlockSpec(memory_space=pltpu.VMEM)] * len(shards),
        out_specs=[pl.BlockSpec(memory_space=pl.ANY)] * len(shards),
        out_shape=[
            jax.ShapeDtypeStruct((depth, 2, 2, s.shape[0], 2 * s.shape[1]), s.dtype) for s in shards
        ],
        scratch_shapes=[
            pltpu.SemaphoreType.DMA((total,)),
            pltpu.SemaphoreType.DMA((total, depth + 2)),
            pltpu.SemaphoreType.DMA((total, depth + 2)),
        ],
        compiler_params=pltpu.CompilerParams(collective_id=cid, has_side_effects=True),
    )(*shards)
    return [o.reshape(-1, o.shape[-1]) for o in outs]


def reduce_kernel(parts, depth, count, shapes, *refs):
    grads, outs = refs[:count], refs[count : 2 * count]
    own, near = refs[2 * count : 3 * count], refs[3 * count : 4 * count]
    mid, side, far, last = (refs[i * count : (i + 1) * count] for i in (4, 5, 6, 7))
    own_sem, send, recv = refs[8 * count :]
    core, x, z, y = place()
    greet(core, x, z, y, depth)
    pending = []

    def push(src, dst, p, lane, target):
        copy = pltpu.make_async_remote_copy(
            src_ref=src,
            dst_ref=dst,
            send_sem=send.at[p, lane],
            recv_sem=recv.at[p, lane],
            device_id=target,
            device_id_type=MESH,
        )
        copy.start()
        pending.append(copy)
        return copy

    def view(p):
        w, start, size, kind = parts[p]
        return w, pl.ds(start, size), shapes[w][1], kind

    state = {}

    def add(left, right):
        return left[...].astype(jnp.float32) + right[...].astype(jnp.float32)

    def stage0(p):
        w, rows, width, kind = view(p)
        local = pltpu.make_async_copy(
            grads[w].at[:, :, core, rows], own[w].at[:, :, rows], own_sem.at[p]
        )
        local.start()
        copy = push(
            grads[w].at[:, :, 1 - core, rows],
            near[w].at[:, :, rows],
            p,
            depth - 1,
            site(1 - core, x, z, y),
        )
        state[p] = (local, copy)

    def stage1(p):
        w, rows, width, kind = view(p)
        local, copy = state[p]
        local.wait()
        copy.wait_recv()

        def body(i, carry):
            mine = own[w].at[i // 2, lax.rem(i, 2), rows]
            mine[...] = add(mine, near[w].at[i // 2, lax.rem(i, 2), rows]).astype(jnp.bfloat16)
            return carry

        lax.fori_loop(0, 2 * depth, body, 0)
        if kind == 0:
            state[p] = push(
                own[w].at[:, :, rows, columns(1 - y, width)],
                mid[w].at[:, :, rows],
                p,
                depth,
                site(core, x, z, 1 - y),
            )
        else:
            state[p] = push(
                own[w].at[:, 1 - x, rows],
                side[w].at[:, rows],
                p,
                depth,
                site(core, 1 - x, z, y),
            )

    def stage2(p):
        w, rows, width, kind = view(p)
        state[p].wait_recv()
        if kind == 0:

            def body(i, carry):
                mine = own[w].at[i // 2, lax.rem(i, 2), rows, columns(y, width)]
                mine[...] = add(mine, mid[w].at[i // 2, lax.rem(i, 2), rows]).astype(jnp.bfloat16)
                return carry

            lax.fori_loop(0, 2 * depth, body, 0)
            state[p] = push(
                own[w].at[:, 1 - x, rows, columns(y, width)],
                far[w].at[:, rows],
                p,
                depth + 1,
                site(core, 1 - x, z, y),
            )
        else:

            def body(i, carry):
                mine = own[w].at[i, x, rows]
                mine[...] = add(mine, side[w].at[i, rows]).astype(jnp.bfloat16)
                return carry

            lax.fori_loop(0, depth, body, 0)
            state[p] = push(
                own[w].at[:, x, rows, columns(1 - y, width)],
                far[w].at[:, rows],
                p,
                depth + 1,
                site(core, x, z, 1 - y),
            )

    def stage3(p):
        w, rows, width, kind = view(p)
        state[p].wait_recv()

        def body(i, carry):
            mine = own[w].at[i, x, rows, columns(y, width)]
            mine[...] = add(mine, far[w].at[i, rows]).astype(jnp.bfloat16)
            return carry

        lax.fori_loop(0, depth, body, 0)
        state[p] = [
            push(
                own[w].at[lax.rem(z + k, depth), x, rows, columns(y, width)],
                last[w].at[k - 1, rows],
                p,
                k - 1,
                site(core, x, lax.rem(z + k, depth), y),
            )
            for k in range(1, depth)
        ]

    def stage4(p):
        w, rows, width, kind = view(p)
        for copy in state[p]:
            copy.wait_recv()
        total = own[w][z, x, rows, columns(y, width)].astype(jnp.float32)
        for k in range(depth - 1):
            total = total + last[w][k, rows].astype(jnp.float32)
        outs[w][rows] = total

    total = len(parts)
    for p in range(total):
        stage0(p)
    for step in range(total // 2 + 4):
        for lag, stage in enumerate((stage1, stage2, stage3, stage4)):
            for p in (2 * (step - lag), 2 * (step - lag) + 1):
                if 0 <= p < total:
                    stage(p)
    for copy in pending:
        copy.wait_send()


def reduce_sum(grads, pieces, cid, depth):
    count = len(grads)
    shapes = [(g.shape[0] // (4 * depth), g.shape[1] // 2) for g in grads]
    parts = split_rows(shapes, pieces)
    total = len(parts)

    def each(form):
        return [pltpu.VMEM(form(r, c), jnp.bfloat16) for r, c in shapes]

    return pl.pallas_call(
        functools.partial(reduce_kernel, parts, depth, count, shapes),
        in_specs=[pl.BlockSpec(memory_space=pl.ANY)] * count,
        out_specs=[pl.BlockSpec(memory_space=pltpu.VMEM)] * count,
        out_shape=[jax.ShapeDtypeStruct(s, jnp.float32) for s in shapes],
        scratch_shapes=each(lambda r, c: (depth, 2, r, 2 * c))
        + each(lambda r, c: (depth, 2, r, 2 * c))
        + each(lambda r, c: (depth, 2, r, c))
        + each(lambda r, c: (depth, r, 2 * c))
        + each(lambda r, c: (depth, r, c))
        + each(lambda r, c: (depth - 1, r, c))
        + [
            pltpu.SemaphoreType.DMA((total,)),
            pltpu.SemaphoreType.DMA((total, depth + 2)),
            pltpu.SemaphoreType.DMA((total, depth + 2)),
        ],
        compiler_params=pltpu.CompilerParams(
            collective_id=cid, has_side_effects=True, vmem_limit_bytes=56 * 1024 * 1024
        ),
    )(*[g.reshape(depth, 2, 2, r, 2 * c) for g, (r, c) in zip(grads, shapes)])


def general_body(
    images,
    cotangent,
    w_qkv,
    w_out,
    w_up,
    w_down,
    gains,
    biases,
    first_qkv,
    first_out,
    first_up,
    first_down,
    first_gains,
    first_biases,
    second_qkv,
    second_out,
    second_up,
    second_down,
    second_gains,
    second_biases,
):
    params = (w_qkv, w_out, w_up, w_down, gains, biases)
    firsts = (first_qkv, first_out, first_up, first_down, first_gains, first_biases)
    seconds = (second_qkv, second_out, second_up, second_down, second_gains, second_biases)
    count, group, width = images.shape
    ways = lax.axis_size("seq")
    blocks = lax.axis_size("dp")
    me = lax.axis_index("seq")
    pad_len = group * ways
    by_image = count % ways == 0
    rows_dp = w_qkv.shape[0]
    cols = w_out.shape[1]
    fold = w_up.shape[1] // cols
    own = gains.shape[1]
    small = jnp.concatenate([gains, biases], axis=0).astype(jnp.bfloat16).T
    lanes = -(-small.shape[1] // LANES) * LANES
    small = jnp.pad(small, ((0, rows_dp - own), (0, lanes - small.shape[1])))
    part_a = jnp.concatenate([w_qkv.astype(jnp.bfloat16), small], axis=1)
    wide_a = lax.all_gather(part_a, ("seq", "dp"), axis=0, tiled=True)
    part_b = jnp.concatenate(
        [
            w_out.astype(jnp.bfloat16),
            w_up.astype(jnp.bfloat16)
            .reshape(rows_dp, fold, cols)
            .transpose(1, 0, 2)
            .reshape(fold * rows_dp, cols),
            w_down.astype(jnp.bfloat16),
        ],
        axis=0,
    )
    part_b, wide_a = lax.optimization_barrier((part_b, wide_a))
    wide_b = lax.all_gather(part_b, ("seq", "dp"), axis=0, tiled=True)
    wide_a = wide_a.reshape(ways, width, part_a.shape[1])
    wide_qkv = jnp.concatenate([wide_a[k, :, : w_qkv.shape[1]] for k in range(ways)], axis=1)
    wide_small = (
        wide_a.reshape(ways, blocks, rows_dp, part_a.shape[1])[
            :, :, :own, w_qkv.shape[1] : w_qkv.shape[1] + 12
        ]
        .astype(jnp.float32)
        .transpose(3, 1, 0, 2)
        .reshape(12, width)
    )
    gain, bias = wide_small[:2], wide_small[2:]
    back_gain = gain
    wide_b = wide_b.reshape(ways, blocks, part_b.shape[0], cols)
    wide_out = wide_b[:, :, :rows_dp].transpose(1, 2, 0, 3).reshape(width, width)
    wide_up = (
        wide_b[:, :, rows_dp : (1 + fold) * rows_dp]
        .reshape(ways, blocks, fold, rows_dp, cols)
        .transpose(1, 3, 0, 2, 4)
        .reshape(width, fold * width)
    )
    wide_down = (
        wide_b[:, :, (1 + fold) * rows_dp :].transpose(1, 2, 0, 3).reshape(fold * width, width)
    )
    back_qkv, back_out, back_up, back_down = wide_qkv, wide_out, wide_up, wide_down
    spot = jnp.arange(group, dtype=jnp.int32)
    if by_image:
        images, cotangent = spread(images), spread(cotangent)
        token_live = jnp.concatenate(
            [lax.rem(me - k + ways, ways) * group + spot for k in range(ways)]
        ) < PATCH_TOK
        key_live = token_live
    else:
        token_live = me * group + spot < PATCH_TOK
        key_live = jnp.arange(pad_len, dtype=jnp.int32) < PATCH_TOK
    query_live = token_live
    key_live = key_live.astype(jnp.float32)
    rows = images.astype(jnp.float32)
    normed_a, inverse_a = normalize(rows)
    hidden_a = (normed_a * gain[0] + bias[0]).astype(jnp.bfloat16)
    mixed = jnp.einsum("icd,de->ice", hidden_a, wide_qkv, preferred_element_type=jnp.float32)
    queries = (mixed[..., :width] + bias[1]).astype(jnp.bfloat16)
    keys = mixed[..., width : 2 * width].astype(jnp.bfloat16)
    values = (mixed[..., 2 * width :] + bias[2]).astype(jnp.bfloat16)
    if by_image:
        keys_all, values_all = keys, values
    else:
        keys_all, values_all = (
            lax.all_gather(keys, "seq", axis=1, tiled=True),
            lax.all_gather(values, "seq", axis=1, tiled=True),
        )
    context = attend(queries, keys_all, values_all, key_live)
    resid = (
        rows
        + jnp.einsum("icd,de->ice", context, wide_out, preferred_element_type=jnp.float32)
        + bias[3]
    )
    normed_b, inverse_b = normalize(resid)
    hidden_b = (normed_b * gain[1] + bias[4]).astype(jnp.bfloat16)
    pre = jnp.einsum("icd,df->icf", hidden_b, wide_up, preferred_element_type=jnp.float32) + bias[
        6:
    ].reshape(-1)
    active = gelu_value(pre).astype(jnp.bfloat16)
    out_images = (
        resid
        + jnp.einsum("icf,fd->icd", active, wide_down, preferred_element_type=jnp.float32)
        + bias[5]
    ).astype(jnp.bfloat16)
    grad_y = cotangent.astype(jnp.float32) * query_live[None, :, None].astype(jnp.float32)
    grad_yb = grad_y.astype(jnp.bfloat16)
    g_down = jnp.einsum("icf,icd->fd", active, grad_yb, preferred_element_type=jnp.float32)
    grad_pre = jnp.einsum(
        "icd,fd->icf", grad_yb, back_down, preferred_element_type=jnp.float32
    ) * gelu_slope(pre)
    grad_preb = grad_pre.astype(jnp.bfloat16)
    g_up = jnp.einsum("icd,icf->df", hidden_b, grad_preb, preferred_element_type=jnp.float32)
    grad_hb = jnp.einsum("icf,df->icd", grad_preb, back_up, preferred_element_type=jnp.float32)
    grad_resid = grad_y + norm_back(grad_hb, normed_b, inverse_b, back_gain[1])
    grad_rb = grad_resid.astype(jnp.bfloat16)
    g_outw = jnp.einsum("icd,ice->de", context, grad_rb, preferred_element_type=jnp.float32)
    grad_ctx = jnp.einsum(
        "ice,de->icd", grad_rb, back_out, preferred_element_type=jnp.float32
    ).astype(jnp.bfloat16)
    grad_q, grad_k, grad_v = attend_back(
        queries,
        keys_all,
        values_all,
        grad_ctx,
        key_live,
        jnp.float32 if by_image else jnp.bfloat16,
    )
    if not by_image:
        grad_k, grad_v = (
            lax.psum_scatter(grad_k, "seq", scatter_dimension=1, tiled=True).astype(jnp.float32),
            lax.psum_scatter(grad_v, "seq", scatter_dimension=1, tiled=True).astype(jnp.float32),
        )
    grad_mixed = jnp.concatenate([grad_q, grad_k, grad_v], axis=-1).astype(jnp.bfloat16)
    g_qkv = jnp.einsum("icd,ice->de", hidden_a, grad_mixed, preferred_element_type=jnp.float32)
    grad_ha = jnp.einsum("ice,de->icd", grad_mixed, back_qkv, preferred_element_type=jnp.float32)
    grad_images = (grad_resid + norm_back(grad_ha, normed_a, inverse_a, back_gain[0])).astype(
        jnp.bfloat16
    )
    g_gains = jnp.stack(
        [jnp.sum(grad_ha * normed_a, axis=(0, 1)), jnp.sum(grad_hb * normed_b, axis=(0, 1))]
    )
    g_biases = jnp.concatenate(
        [
            jnp.stack(
                [
                    jnp.sum(grad_ha, axis=(0, 1)),
                    jnp.sum(grad_q, axis=(0, 1)),
                    jnp.sum(grad_v, axis=(0, 1)),
                    jnp.sum(grad_resid, axis=(0, 1)),
                    jnp.sum(grad_hb, axis=(0, 1)),
                    jnp.sum(grad_y, axis=(0, 1)),
                ]
            ),
            jnp.sum(grad_pre, axis=(0, 1)).reshape(-1, width),
        ],
        axis=0,
    )
    if by_image:
        out_images, grad_images = unspread(out_images), unspread(grad_images)
    send_a = jnp.concatenate(
        [
            g_outw.astype(jnp.bfloat16).reshape(blocks, rows_dp, width),
            g_up.astype(jnp.bfloat16)
            .reshape(blocks, rows_dp, ways, fold, cols)
            .transpose(0, 3, 1, 2, 4)
            .reshape(blocks, fold * rows_dp, width),
            g_down.astype(jnp.bfloat16).reshape(blocks, fold * rows_dp, width),
        ],
        axis=1,
    ).reshape(-1, width)
    part = lax.psum_scatter(send_a, "dp", scatter_dimension=0, tiled=True)
    total_a = sum_over_seq(part, 1)
    g_small = jnp.concatenate([g_gains, g_biases], axis=0).astype(jnp.bfloat16).T
    g_small = jnp.pad(g_small, ((0, 0), (0, lanes - g_small.shape[1])))
    send_b = jnp.concatenate([g_qkv.astype(jnp.bfloat16), g_small], axis=1)
    part, _ = lax.optimization_barrier((send_b, part))
    part = lax.psum_scatter(part, "dp", scatter_dimension=0, tiled=True)
    total_qkv = sum_over_seq(part[:, : g_qkv.shape[1]], 1)
    total_small = sum_over_seq(part[:, g_qkv.shape[1] :], 0)[:, :12].T
    totals = (
        total_qkv,
        total_a[:rows_dp],
        total_a[rows_dp : (1 + fold) * rows_dp]
        .reshape(fold, rows_dp, cols)
        .transpose(1, 0, 2)
        .reshape(rows_dp, fold * cols),
        total_a[(1 + fold) * rows_dp :],
        total_small[:2],
        total_small[2:],
    )
    updated = [
        adamw(param, grad, first, second)
        for param, grad, first, second in zip(params, totals, firsts, seconds)
    ]
    news = tuple((entry[0] for entry in updated))
    new_firsts = tuple((entry[1] for entry in updated))
    new_seconds = tuple((entry[2] for entry in updated))
    return (
        out_images,
        grad_images,
        totals[0],
        totals[1],
        totals[2],
        totals[3],
        totals[4],
        totals[5],
        news[0],
        news[1],
        news[2],
        news[3],
        news[4],
        news[5],
        new_firsts[0],
        new_firsts[1],
        new_firsts[2],
        new_firsts[3],
        new_firsts[4],
        new_firsts[5],
        new_seconds[0],
        new_seconds[1],
        new_seconds[2],
        new_seconds[3],
        new_seconds[4],
        new_seconds[5],
    )


def is_paired(mesh):
    return mesh.shape["seq"] == 2 and mesh.shape["dp"] % 4 == 0


def head_lanes(rows):
    lane = lax.broadcasted_iota(jnp.int32, (rows, LANES), 1)
    return lane // HEAD_DIM, lax.rem(lane, HEAD_DIM)


def three_terms(spot, value):
    high = value.astype(jnp.bfloat16)
    rest = value - high.astype(jnp.float32)
    middle = rest.astype(jnp.bfloat16)
    low = (rest - middle.astype(jnp.float32)).astype(jnp.bfloat16)
    zero = jnp.zeros((), jnp.bfloat16)
    return jnp.where(
        spot == 0, high, jnp.where(spot == 1, middle, jnp.where(spot == 2, low, zero))
    )


def dead_lane(spot, live):
    floor = jnp.where(live > 0.5, 0.0, -1e30)
    ones = jnp.where(spot < 3, 1.0, jnp.where(spot == 3, floor, 0.0))
    return ones.astype(jnp.bfloat16)


def attend_mixed_kernel(q_ref, k_ref, v_ref, live_ref, ctx_ref, lse_ref):
    q, k, v = q_ref[0], k_ref[0], v_ref[0]
    half, spot = head_lanes(q.shape[0])
    q = q * jnp.asarray(HEAD_DIM**-0.5, q.dtype)
    side_q = (spot == 3).astype(jnp.float32).astype(jnp.bfloat16)
    side_k = dead_lane(spot, live_ref[...])
    total = jnp.zeros(q.shape, jnp.float32)
    lse = jnp.zeros(q.shape, jnp.float32)
    for h in range(LANES // HEAD_DIM):
        mask = half == h
        scores = dot(jnp.where(mask, q, side_q), jnp.where(mask, k, side_k), NT)
        top = jnp.max(scores, axis=-1, keepdims=True)
        weights = jnp.exp(scores - top)
        denom = jnp.sum(weights, axis=-1, keepdims=True)
        total = jnp.where(mask, dot(weights.astype(jnp.bfloat16), v, NN) * (1.0 / denom), total)
        lse = jnp.where(mask, lse, top + jnp.log(denom))
    ctx_ref[0] = total.astype(jnp.bfloat16)
    lse_ref[0] = lse


def mixed_specs(rows, heads):
    return [
        pl.BlockSpec((1, rows, LANES), lambda i, h, k=k: (i, 0, h + k * heads)) for k in range(3)
    ]


def attend_mixed(mixed, live):
    count, rows, triple = mixed.shape
    width = triple // 3
    heads = width // LANES
    specs = mixed_specs(rows, heads)
    pairs = count * rows * rows * width
    return pl.pallas_call(
        attend_mixed_kernel,
        grid=(count, heads),
        in_specs=specs + [pl.BlockSpec((rows, 1), lambda i, h: (0, 0))],
        out_specs=[specs[0], specs[0]],
        out_shape=[
            jax.ShapeDtypeStruct((count, rows, width), jnp.bfloat16),
            jax.ShapeDtypeStruct((count, rows, width), jnp.float32),
        ],
        cost_estimate=pl.CostEstimate(
            flops=8 * pairs, bytes_accessed=2 * mixed.size, transcendentals=pairs // HEAD_DIM
        ),
        compiler_params=pltpu.CompilerParams(vmem_limit_bytes=48 * 1024 * 1024),
    )(mixed, mixed, mixed, live.reshape(rows, 1))


def attend_back_mixed_kernel(
    q_ref, k_ref, v_ref, g_ref, ctx_ref, lse_ref, live_ref, dm_ref, sum_ref
):
    q, k, v, g = q_ref[0], k_ref[0], v_ref[0], g_ref[0]
    scale = HEAD_DIM**-0.5
    half, spot = head_lanes(q.shape[0])
    q = q * jnp.asarray(scale, q.dtype)
    one = (spot == 3).astype(jnp.float32).astype(jnp.bfloat16)
    side_q = three_terms(spot, -lse_ref[0]) + one
    side_k = dead_lane(spot, live_ref[...])
    side_v = (spot < 3).astype(jnp.float32).astype(jnp.bfloat16)
    agree = g.astype(jnp.float32) * ctx_ref[0].astype(jnp.float32)
    dq = jnp.zeros(q.shape, jnp.float32)
    dk = jnp.zeros(q.shape, jnp.float32)
    dv = jnp.zeros(q.shape, jnp.float32)
    for h in range(LANES // HEAD_DIM):
        mask = half == h
        delta = jnp.sum(jnp.where(mask, agree, 0.0), axis=1, keepdims=True)
        q_h = jnp.where(mask, q, side_q)
        k_h = jnp.where(mask, k, side_k)
        v_h = jnp.where(mask, v, side_v)
        g_h = jnp.where(mask, g, three_terms(spot, jnp.broadcast_to(-delta, q.shape)))
        probs = jnp.exp(dot(k_h, q_h, NT))
        grad_scores = (probs * dot(v_h, g_h, NT)).astype(jnp.bfloat16)
        dv = jnp.where(mask, dot(probs.astype(jnp.bfloat16), g, NN), dv)
        dk = jnp.where(mask, dot(grad_scores, q, NN), dk)
        dq = jnp.where(mask, dot(grad_scores, k, TN), dq)
    image, head = pl.program_id(0), pl.program_id(1)
    width = dm_ref.shape[2] // 3

    @pl.when(jnp.logical_and(image == 0, head == 0))
    def _():
        sum_ref[...] = jnp.zeros_like(sum_ref)

    for n, part in enumerate((dq * scale, dk, dv)):
        where = pl.ds(pl.multiple_of(n * width + head * LANES, LANES), LANES)
        dm_ref[0, :, where] = part.astype(jnp.bfloat16)
        sum_ref[:, where] += jnp.sum(part, axis=0, keepdims=True)


def attend_back_mixed(mixed, grad_ctx, context, lse, live):
    count, rows, triple = mixed.shape
    width = triple // 3
    heads = width // LANES
    specs = mixed_specs(rows, heads)
    pairs = count * rows * rows * width
    return pl.pallas_call(
        attend_back_mixed_kernel,
        grid=(count, heads),
        in_specs=specs + [specs[0]] * 3 + [pl.BlockSpec((rows, 1), lambda i, h: (0, 0))],
        out_specs=[
            pl.BlockSpec((1, rows, triple), lambda i, h: (i, 0, 0)),
            pl.BlockSpec((1, triple), lambda i, h: (0, 0)),
        ],
        out_shape=[
            jax.ShapeDtypeStruct(mixed.shape, jnp.bfloat16),
            jax.ShapeDtypeStruct((1, triple), jnp.float32),
        ],
        cost_estimate=pl.CostEstimate(
            flops=20 * pairs, bytes_accessed=4 * mixed.size, transcendentals=pairs // HEAD_DIM
        ),
        compiler_params=pltpu.CompilerParams(vmem_limit_bytes=56 * 1024 * 1024),
    )(mixed, mixed, mixed, grad_ctx, context, lse, live.reshape(rows, 1))


def small_kernel(slots, own, lanes, *refs):
    rows, out_ref, stack = refs[:-2], refs[-2], refs[-1]
    stack[...] = jnp.zeros_like(stack)
    out_ref[...] = jnp.zeros_like(out_ref)
    width = stack.shape[1]
    at = 0
    for ref in rows:
        for start in range(0, ref.shape[1], width):
            stack[at : at + 1] = ref[:, start : start + width]
            at += 1
    filled = stack[...].astype(jnp.bfloat16)
    for slot in range(slots):
        piece = filled[:, slot * own : (slot + 1) * own]
        out_ref[slot // 2, :, (slot % 2) * lanes : (slot % 2) * lanes + own] = piece


def pack_small(rows, blocks, tall, own, lanes):
    width = rows[0].shape[1]
    return pl.pallas_call(
        functools.partial(small_kernel, 2 * blocks, own, lanes),
        out_shape=jax.ShapeDtypeStruct((blocks, tall, 2 * lanes), jnp.bfloat16),
        scratch_shapes=[pltpu.VMEM((tall, width), jnp.float32)],
    )(*rows).reshape(blocks * tall, 2 * lanes)


def product(a, b, dims=NN):
    return lax.dot_general(a, b, dims, preferred_element_type=jnp.float32)


def sum_rows(rows):
    return jnp.sum(rows, axis=0, keepdims=True)


def fast_body(images, cotangent, *rest):
    params, firsts, seconds = rest[:6], rest[6:12], rest[12:]
    w_qkv, w_out, w_up, w_down, gains, biases = params
    count, group, width = images.shape
    ways = lax.axis_size("seq")
    blocks = lax.axis_size("dp")
    depth = blocks // 4
    me = lax.axis_index("seq")
    narrow = jnp.bfloat16
    vectors = gains.shape[0] + biases.shape[0]
    own = gains.shape[1]
    lanes = -(-own // LANES) * LANES
    tall = -(-vectors // 32) * 32
    small = jnp.concatenate([gains, biases], axis=0).astype(narrow)
    small = jnp.pad(small, ((0, tall - vectors), (0, lanes - own)))
    images, cotangent = spread(images), spread(cotangent)
    each, length = images.shape[:2]
    wide_qkv, wide_small, wide_out, wide_up, wide_down = gather(
        [w_qkv.astype(narrow), small, w_out.astype(narrow), w_up.astype(narrow), w_down.astype(narrow)],
        (4, 2, 2, 4, 4),
        1,
        depth,
    )
    wide_small = (
        wide_small.reshape(blocks, tall, ways, lanes)[:, :vectors, :, :own]
        .astype(jnp.float32)
        .transpose(1, 0, 2, 3)
        .reshape(vectors, width)
    )
    gain, bias = wide_small[: gains.shape[0]], wide_small[gains.shape[0] :]
    spot = jnp.arange(group, dtype=jnp.int32)
    live = jnp.concatenate(
        [lax.rem(me - k + ways, ways) * group + spot for k in range(ways)]
    ) < PATCH_TOK
    key_live = live.astype(jnp.float32)
    rows = images.reshape(each * length, width).astype(jnp.float32)
    normed_a, inverse_a = normalize(rows)
    hidden_a = (normed_a * gain[0] + bias[0]).astype(narrow)
    shift = jnp.concatenate([bias[1], jnp.zeros_like(bias[1]), bias[2]])
    mixed = (product(hidden_a, wide_qkv) + shift).astype(narrow).reshape(each, length, 3 * width)
    context, lse = attend_mixed(mixed, key_live)
    context = context.reshape(each * length, width)
    resid = rows + product(context, wide_out) + bias[3]
    normed_b, inverse_b = normalize(resid)
    hidden_b = (normed_b * gain[1] + bias[4]).astype(narrow)
    pre = product(hidden_b, wide_up) + bias[6:].reshape(-1)
    active = gelu_value(pre).astype(narrow)
    out_images = (resid + product(active, wide_down) + bias[5]).astype(narrow)
    grad_y = cotangent.astype(jnp.float32) * live[None, :, None].astype(jnp.float32)
    grad_y = grad_y.reshape(each * length, width)
    grad_yb = grad_y.astype(narrow)
    grad_yb, out_images = lax.optimization_barrier((grad_yb, out_images))
    out_images = unspread(out_images.reshape(each, length, width))
    g_down = product(active, grad_yb, TN)
    grad_pre = product(grad_yb, wide_down, NT) * gelu_slope(pre)
    grad_preb = grad_pre.astype(narrow)
    g_up = product(hidden_b, grad_preb, TN)
    grad_hb = product(grad_preb, wide_up, NT)
    grad_resid = grad_y + norm_back(grad_hb, normed_b, inverse_b, gain[1])
    grad_rb = grad_resid.astype(narrow)
    g_outw = product(context, grad_rb, TN)
    grad_ctx = product(grad_rb, wide_out, NT).astype(narrow).reshape(each, length, width)
    grad_mixed, mixed_sum = attend_back_mixed(
        mixed, grad_ctx, context.reshape(each, length, width), lse, key_live
    )
    grad_mixed = grad_mixed.reshape(each * length, 3 * width)
    g_qkv = product(hidden_a, grad_mixed, TN)
    grad_ha = product(grad_mixed, wide_qkv, NT)
    grad_images = (grad_resid + norm_back(grad_ha, normed_a, inverse_a, gain[0])).astype(narrow)
    grad_images = unspread(grad_images.reshape(each, length, width))
    g_small = pack_small(
        [
            sum_rows(grad_ha * normed_a),
            sum_rows(grad_hb * normed_b),
            sum_rows(grad_ha),
            mixed_sum[:, :width],
            mixed_sum[:, 2 * width :],
            sum_rows(grad_resid),
            sum_rows(grad_hb),
            sum_rows(grad_y),
            sum_rows(grad_pre),
        ],
        blocks,
        tall,
        own,
        lanes,
    )
    t_down, t_up, t_out, t_qkv, t_small = reduce_sum(
        [g.astype(narrow) for g in (g_down, g_up, g_outw, g_qkv, g_small)],
        (4, 4, 2, 4, 2),
        2,
        depth,
    )
    t_small = t_small[:vectors, :own]
    totals = (t_qkv, t_out, t_up, t_down, t_small[: gains.shape[0]], t_small[gains.shape[0] :])
    updated = [
        adamw(param, grad, first, second)
        for param, grad, first, second in zip(params, totals, firsts, seconds)
    ]
    return (
        out_images,
        grad_images,
        *totals,
        *(entry[0] for entry in updated),
        *(entry[1] for entry in updated),
        *(entry[2] for entry in updated),
    )


def solution(mesh):
    body = fast_body if is_paired(mesh) else general_body
    return jax.shard_map(
        body,
        mesh=mesh,
        in_specs=(
            P("dp", "seq", None),
            P("dp", "seq", None),
            P("dp", "seq"),
            P("dp", "seq"),
            P("dp", "seq"),
            P("dp", "seq"),
            P(None, ("dp", "seq")),
            P(None, ("dp", "seq")),
            P("dp", "seq"),
            P("dp", "seq"),
            P("dp", "seq"),
            P("dp", "seq"),
            P(None, ("dp", "seq")),
            P(None, ("dp", "seq")),
            P("dp", "seq"),
            P("dp", "seq"),
            P("dp", "seq"),
            P("dp", "seq"),
            P(None, ("dp", "seq")),
            P(None, ("dp", "seq")),
        ),
        out_specs=(
            P("dp", "seq", None),
            P("dp", "seq", None),
            P("dp", "seq"),
            P("dp", "seq"),
            P("dp", "seq"),
            P("dp", "seq"),
            P(None, ("dp", "seq")),
            P(None, ("dp", "seq")),
            P("dp", "seq"),
            P("dp", "seq"),
            P("dp", "seq"),
            P("dp", "seq"),
            P(None, ("dp", "seq")),
            P(None, ("dp", "seq")),
            P("dp", "seq"),
            P("dp", "seq"),
            P("dp", "seq"),
            P("dp", "seq"),
            P(None, ("dp", "seq")),
            P(None, ("dp", "seq")),
            P("dp", "seq"),
            P("dp", "seq"),
            P("dp", "seq"),
            P("dp", "seq"),
            P(None, ("dp", "seq")),
            P(None, ("dp", "seq")),
        ),
        check_vma=False,
    )
```

```python
import functools

import jax
import jax.numpy as jnp
from jax import lax
from jax.experimental import pallas as pl
from jax.experimental.pallas import tpu as pltpu
from jax.sharding import PartitionSpec as P

HEAD_DIM = 64
PATCH_TOK = 577
STEP = 5


def normalize(rows):
    center = rows - jnp.mean(rows, axis=-1, keepdims=True)
    inverse = lax.rsqrt(jnp.mean(center * center, axis=-1, keepdims=True) + 1e-06)
    return (center * inverse, inverse)


def norm_back(grad_out, normed, inverse, gain):
    scaled = grad_out * gain
    return inverse * (
        scaled
        - jnp.mean(scaled, axis=-1, keepdims=True)
        - normed * jnp.mean(scaled * normed, axis=-1, keepdims=True)
    )


def gelu_value(pre):
    return pre * 0.5 * (1.0 + lax.erf(pre * 0.7071067811865476))


def gelu_slope(pre):
    return (
        0.5 * (1.0 + lax.erf(pre * 0.7071067811865476))
        + pre * jnp.exp(-0.5 * pre * pre) * 0.3989422804014327
    )


def adamw(param, grad, first, second):
    first_new = 0.9 * first + 0.1 * grad
    second_new = 0.95 * second + 0.05 * grad * grad
    step_size = first_new / (1.0 - 0.9**STEP) / (jnp.sqrt(second_new / (1.0 - 0.95**STEP)) + 1e-08)
    return (param - 0.004 * (step_size + 0.05 * param), first_new, second_new)


LANES = 128
NT = (((1,), (1,)), ((), ()))
NN = (((1,), (0,)), ((), ()))
TN = (((0,), (0,)), ((), ()))


def dot(a, b, dims):
    return lax.dot_general(a, b, dims, preferred_element_type=jnp.float32)


def head_masks(rows, dtype):
    lane = lax.broadcasted_iota(jnp.int32, (rows, LANES), 1)
    return [
        ((lane >= h * HEAD_DIM) & (lane < (h + 1) * HEAD_DIM)) for h in range(LANES // HEAD_DIM)
    ]


def attend_kernel(q_ref, k_ref, v_ref, live_ref, ctx_ref):
    q, k, v = q_ref[0], k_ref[0], v_ref[0]
    live = live_ref[...] > 0.5
    total = jnp.zeros(q.shape, jnp.float32)
    zero = jnp.zeros_like(q)
    for mask in head_masks(q.shape[0], q.dtype):
        scores = dot(jnp.where(mask, q, zero), k, NT) * (HEAD_DIM**-0.5)
        scores = jnp.where(live, scores, -1e30)
        top = jnp.max(scores, axis=-1, keepdims=True)
        weights = jnp.exp(scores - top)
        denom = jnp.sum(weights, axis=-1, keepdims=True)
        probs = (weights * (1.0 / denom)).astype(jnp.bfloat16)
        total = jnp.where(mask, dot(probs, v, NN), total)
    ctx_ref[0] = total.astype(jnp.bfloat16)


def attend_back_kernel(q_ref, k_ref, v_ref, g_ref, live_ref, dq_ref, dk_ref, dv_ref):
    q, k, v, g = q_ref[0], k_ref[0], v_ref[0], g_ref[0]
    live = live_ref[...] > 0.5
    zero_q = jnp.zeros_like(q)
    zero_k = jnp.zeros_like(k)
    dq = jnp.zeros(q.shape, jnp.float32)
    dk = jnp.zeros(k.shape, jnp.float32)
    dv = jnp.zeros(k.shape, jnp.float32)
    masks_q = head_masks(q.shape[0], q.dtype)
    masks_k = head_masks(k.shape[0], k.dtype)
    for mask, mask_k in zip(masks_q, masks_k):
        q_h = jnp.where(mask, q, zero_q)
        g_h = jnp.where(mask, g, zero_q)
        k_h = jnp.where(mask_k, k, zero_k)
        scores = dot(k, q_h, NT) * (HEAD_DIM**-0.5)
        scores = jnp.where(live, scores, -1e30)
        top = jnp.max(scores, axis=0, keepdims=True)
        weights = jnp.exp(scores - top)
        denom = jnp.sum(weights, axis=0, keepdims=True)
        probs = weights * (1.0 / denom)
        grad_probs = dot(v, g_h, NT)
        delta = jnp.sum(probs * grad_probs, axis=0, keepdims=True)
        grad_scores = (probs * (grad_probs - delta) * (HEAD_DIM**-0.5)).astype(jnp.bfloat16)
        dv = dv + dot(probs.astype(jnp.bfloat16), g_h, NN)
        dk = dk + dot(grad_scores, q_h, NN)
        dq = dq + dot(grad_scores, k_h, TN)
    dq_ref[0] = dq
    dk_ref[0] = dk.astype(dk_ref.dtype)
    dv_ref[0] = dv.astype(dv_ref.dtype)


def attend(queries, keys, values, live):
    count, rows, width = queries.shape
    length = keys.shape[1]
    q_spec = pl.BlockSpec((1, rows, LANES), lambda i, h: (i, 0, h))
    k_spec = pl.BlockSpec((1, length, LANES), lambda i, h: (i, 0, h))
    pairs = count * rows * length * width
    return pl.pallas_call(
        attend_kernel,
        grid=(count, width // LANES),
        in_specs=[q_spec, k_spec, k_spec, pl.BlockSpec((1, length), lambda i, h: (0, 0))],
        out_specs=q_spec,
        out_shape=jax.ShapeDtypeStruct(queries.shape, jnp.bfloat16),
        cost_estimate=pl.CostEstimate(
            flops=8 * pairs, bytes_accessed=8 * queries.size, transcendentals=pairs // HEAD_DIM
        ),
        compiler_params=pltpu.CompilerParams(vmem_limit_bytes=48 * 1024 * 1024),
    )(queries, keys, values, live.reshape(1, length))


def attend_back(queries, keys, values, grad_ctx, live, back_dtype):
    count, rows, width = queries.shape
    length = keys.shape[1]
    q_spec = pl.BlockSpec((1, rows, LANES), lambda i, h: (i, 0, h))
    k_spec = pl.BlockSpec((1, length, LANES), lambda i, h: (i, 0, h))
    pairs = count * rows * length * width
    return pl.pallas_call(
        attend_back_kernel,
        grid=(count, width // LANES),
        in_specs=[q_spec, k_spec, k_spec, q_spec, pl.BlockSpec((length, 1), lambda i, h: (0, 0))],
        out_specs=[q_spec, k_spec, k_spec],
        out_shape=[
            jax.ShapeDtypeStruct(queries.shape, jnp.float32),
            jax.ShapeDtypeStruct(keys.shape, back_dtype),
            jax.ShapeDtypeStruct(keys.shape, back_dtype),
        ],
        cost_estimate=pl.CostEstimate(
            flops=20 * pairs, bytes_accessed=20 * queries.size, transcendentals=pairs // HEAD_DIM
        ),
        compiler_params=pltpu.CompilerParams(vmem_limit_bytes=56 * 1024 * 1024),
    )(queries, keys, values, grad_ctx, live.reshape(length, 1))


def shift_by(step, ways):
    return [(i, (i + step) % ways) for i in range(ways)]


def spread(tokens):
    ways = lax.axis_size("seq")
    me = lax.axis_index("seq")
    each = tokens.shape[0] // ways
    parts = [lax.dynamic_slice_in_dim(tokens, me * each, each, 0)]
    for step in range(1, ways):
        target = lax.rem(me + step, ways)
        piece = lax.dynamic_slice_in_dim(tokens, target * each, each, 0)
        parts.append(lax.ppermute(piece, "seq", shift_by(step, ways)))
    return jnp.concatenate(parts, axis=1)


def unspread(tokens):
    ways = lax.axis_size("seq")
    me = lax.axis_index("seq")
    each, length, width = tokens.shape
    group = length // ways
    result = jnp.zeros((each * ways, group, width), tokens.dtype)
    for step in range(ways):
        piece = tokens[:, step * group : (step + 1) * group]
        if step:
            piece = lax.ppermute(piece, "seq", shift_by(-step, ways))
        source = lax.rem(me + step, ways)
        result = lax.dynamic_update_slice_in_dim(result, piece, source * each, 0)
    return result


def sum_over_seq(terms, axis):
    ways = lax.axis_size("seq")
    me = lax.axis_index("seq")
    size = terms.shape[axis] // ways
    total = lax.dynamic_slice_in_dim(terms, me * size, size, axis).astype(jnp.float32)
    for step in range(1, ways):
        target = lax.rem(me + step, ways)
        piece = lax.dynamic_slice_in_dim(terms, target * size, size, axis)
        total = total + lax.ppermute(piece, "seq", shift_by(step, ways)).astype(jnp.float32)
    return total


MESH = pl.DeviceIdType.MESH


def place():
    d = lax.axis_index("dp")
    return lax.rem(d, 2), lax.rem(d // 2, 2), d // 4, lax.axis_index("seq")


def greet(core, x, z, y, depth):
    barrier = pltpu.get_barrier_semaphore()
    others = [site(core, x, lax.rem(z + k, depth), y) for k in range(1, depth)]
    others += [site(core, 1 - x, z, y), site(core, x, z, 1 - y), site(1 - core, x, z, y)]
    for other in others:
        pl.semaphore_signal(barrier, inc=1, device_id=other, device_id_type=MESH)
    pl.semaphore_wait(barrier, len(others))


def site(core, x, z, y):
    return {"dp": (z * 2 + x) * 2 + core, "seq": y}


def columns(index, size):
    return pl.ds(pl.multiple_of(index * size, LANES), size)


def gather_kernel(parts, depth, count, *refs):
    shards, outs = refs[:count], refs[count : 2 * count]
    own_sem, send, recv = refs[2 * count :]
    core, x, z, y = place()
    greet(core, x, z, y, depth)
    pending = []

    def push(src, dst, p, lane, target):
        copy = pltpu.make_async_remote_copy(
            src_ref=src,
            dst_ref=dst,
            send_sem=send.at[p, lane],
            recv_sem=recv.at[p, lane],
            device_id=target,
            device_id_type=MESH,
        )
        copy.start()
        pending.append(copy)
        return copy

    def view(p):
        w, start, size, kind = parts[p]
        return shards[w].at[start : start + size], outs[w], pl.ds(start, size), shards[w].shape[1], kind

    state = {}

    def stage0(p):
        src, out, rows, width, kind = view(p)
        mine = out.at[z, x, core, rows, columns(y, width)]
        local = pltpu.make_async_copy(src, mine, own_sem.at[p])
        local.start()
        if kind == 2:
            state[p] = [local, push(src, mine, p, depth - 1, site(core, 1 - x, z, y))]
            return
        state[p] = [local] + [
            push(src, mine, p, k - 1, site(core, x, lax.rem(z + k, depth), y))
            for k in range(1, depth)
        ]

    def stage1(p):
        src, out, rows, width, kind = view(p)
        state[p][0].wait()
        for copy in state[p][1:]:
            copy.wait_recv()
        if kind == 2:
            block = out.at[z, :, core, rows, columns(y, width)]
            state[p] = push(block, block, p, depth, site(core, x, z, 1 - y))
            return
        block = out.at[:, x, core, rows, columns(y, width)]
        target = site(core, 1 - x, z, y) if kind == 0 else site(core, x, z, 1 - y)
        state[p] = push(block, block, p, depth - 1, target)

    def stage2(p):
        src, out, rows, width, kind = view(p)
        state[p].wait_recv()
        if kind == 2:
            block = out.at[z, :, core, rows, :]
            state[p] = [
                push(block, block, p, k - 1, site(core, x, lax.rem(z + k, depth), y))
                for k in range(1, depth)
            ]
            return
        if kind == 0:
            block = out.at[:, :, core, rows, columns(y, width)]
            state[p] = push(block, block, p, depth, site(core, x, z, 1 - y))
        else:
            block = out.at[:, x, core, rows, :]
            state[p] = push(block, block, p, depth, site(core, 1 - x, z, y))

    def stage3(p):
        src, out, rows, width, kind = view(p)
        for copy in state[p] if kind == 2 else [state[p]]:
            copy.wait_recv()
        block = out.at[:, :, core, rows, :]
        state[p] = push(block, block, p, depth + 1, site(1 - core, x, z, y))

    def stage4(p):
        state[p].wait_recv()

    in_steps(parts, (stage0, stage1, stage2, stage3, stage4), {1: 0, 2: 1, 3: 99, 4: 99})
    for copy in pending:
        copy.wait_send()


def in_steps(parts, stages, when):
    early = [p for p, part in enumerate(parts) if part[3] == 2]
    usual = [p for p, part in enumerate(parts) if part[3] != 2]
    for p in early + usual:
        stages[0](p)
    steps = -(-len(usual) // 2) + 3
    for step in range(steps):
        for lag, stage in enumerate(stages[1:]):
            if min(when[lag + 1], steps - 1) == step and when[lag + 1] < 50:
                for p in early:
                    stage(p)
            first = 2 * (step - lag)
            for p in usual[max(first, 0) : max(first + 2, 0)]:
                stage(p)
    for lag, stage in enumerate(stages[1:]):
        if when[lag + 1] >= 50:
            for p in early:
                stage(p)


def split_rows(shapes, pieces):
    parts = []
    for w, (shape, n) in enumerate(zip(shapes, pieces)):
        if n:
            size = shape[0] // n
            parts += [(w, i * size, size, i % 2) for i in range(n)]
            continue
        extra = shape[0] * 3 // 16
        half = (shape[0] - 2 * extra) // 2
        big = -(-half // 32) * 16
        start = 0
        for size, kind in ((extra, 2), (extra, 2), (big, 0), (big, 1), (half - big, 0), (half - big, 1)):
            parts.append((w, start, size, kind))
            start += size
    return parts


def gather(shards, pieces, cid, depth):
    parts = split_rows([s.shape for s in shards], pieces)
    total = len(parts)
    outs = pl.pallas_call(
        functools.partial(gather_kernel, parts, depth, len(shards)),
        in_specs=[pl.BlockSpec(memory_space=pltpu.VMEM)] * len(shards),
        out_specs=[pl.BlockSpec(memory_space=pl.ANY)] * len(shards),
        out_shape=[
            jax.ShapeDtypeStruct((depth, 2, 2, s.shape[0], 2 * s.shape[1]), s.dtype) for s in shards
        ],
        scratch_shapes=[
            pltpu.SemaphoreType.DMA((total,)),
            pltpu.SemaphoreType.DMA((total, depth + 2)),
            pltpu.SemaphoreType.DMA((total, depth + 2)),
        ],
        compiler_params=pltpu.CompilerParams(collective_id=cid, has_side_effects=True),
    )(*shards)
    return [o.reshape(-1, o.shape[-1]) for o in outs]


def reduce_kernel(parts, depth, count, shapes, *refs):
    grads, outs = refs[:count], refs[count : 2 * count]
    own, near = refs[2 * count : 3 * count], refs[3 * count : 4 * count]
    mid, side, far, last, ring = (refs[i * count : (i + 1) * count] for i in (4, 5, 6, 7, 8))
    own_sem, send, recv = refs[9 * count :]
    core, x, z, y = place()
    greet(core, x, z, y, depth)
    pending = []

    def push(src, dst, p, lane, target):
        copy = pltpu.make_async_remote_copy(
            src_ref=src,
            dst_ref=dst,
            send_sem=send.at[p, lane],
            recv_sem=recv.at[p, lane],
            device_id=target,
            device_id_type=MESH,
        )
        copy.start()
        pending.append(copy)
        return copy

    def view(p):
        w, start, size, kind = parts[p]
        return w, pl.ds(start, size), shapes[w][1], kind

    state = {}

    def add(left, right):
        return left[...].astype(jnp.float32) + right[...].astype(jnp.float32)

    def stage0(p):
        w, rows, width, kind = view(p)
        local = pltpu.make_async_copy(
            grads[w].at[:, :, core, rows], own[w].at[:, :, rows], own_sem.at[p]
        )
        local.start()
        copy = push(
            grads[w].at[:, :, 1 - core, rows],
            near[w].at[:, :, rows],
            p,
            depth - 1,
            site(1 - core, x, z, y),
        )
        state[p] = (local, copy)

    def stage1(p):
        w, rows, width, kind = view(p)
        local, copy = state[p]
        local.wait()
        copy.wait_recv()

        def body(i, carry):
            mine = own[w].at[i // 2, lax.rem(i, 2), rows]
            mine[...] = add(mine, near[w].at[i // 2, lax.rem(i, 2), rows]).astype(jnp.bfloat16)
            return carry

        lax.fori_loop(0, 2 * depth, body, 0)
        if kind == 2:
            state[p] = [
                push(
                    own[w].at[lax.rem(z + k, depth), :, rows],
                    ring[w].at[k - 1, :, rows],
                    p,
                    k - 1,
                    site(core, x, lax.rem(z + k, depth), y),
                )
                for k in range(1, depth)
            ]
        elif kind == 0:
            state[p] = push(
                own[w].at[:, :, rows, columns(1 - y, width)],
                mid[w].at[:, :, rows],
                p,
                depth,
                site(core, x, z, 1 - y),
            )
        else:
            state[p] = push(
                own[w].at[:, 1 - x, rows],
                side[w].at[:, rows],
                p,
                depth,
                site(core, 1 - x, z, y),
            )

    def stage2(p):
        w, rows, width, kind = view(p)
        for copy in state[p] if kind == 2 else [state[p]]:
            copy.wait_recv()
        if kind == 2:

            def body(i, carry):
                mine = own[w].at[z, i, rows]
                value = mine[...].astype(jnp.float32)
                for k in range(depth - 1):
                    value = value + ring[w][k, i, rows].astype(jnp.float32)
                mine[...] = value.astype(jnp.bfloat16)
                return carry

            lax.fori_loop(0, 2, body, 0)
            state[p] = push(
                own[w].at[z, :, rows, columns(1 - y, width)],
                mid[w].at[0, :, rows],
                p,
                depth,
                site(core, x, z, 1 - y),
            )
        elif kind == 0:

            def body(i, carry):
                mine = own[w].at[i // 2, lax.rem(i, 2), rows, columns(y, width)]
                mine[...] = add(mine, mid[w].at[i // 2, lax.rem(i, 2), rows]).astype(jnp.bfloat16)
                return carry

            lax.fori_loop(0, 2 * depth, body, 0)
            state[p] = push(
                own[w].at[:, 1 - x, rows, columns(y, width)],
                far[w].at[:, rows],
                p,
                depth + 1,
                site(core, 1 - x, z, y),
            )
        else:

            def body(i, carry):
                mine = own[w].at[i, x, rows]
                mine[...] = add(mine, side[w].at[i, rows]).astype(jnp.bfloat16)
                return carry

            lax.fori_loop(0, depth, body, 0)
            state[p] = push(
                own[w].at[:, x, rows, columns(1 - y, width)],
                far[w].at[:, rows],
                p,
                depth + 1,
                site(core, x, z, 1 - y),
            )

    def stage3(p):
        w, rows, width, kind = view(p)
        state[p].wait_recv()
        if kind == 2:

            def body(i, carry):
                mine = own[w].at[z, i, rows, columns(y, width)]
                mine[...] = add(mine, mid[w].at[0, i, rows]).astype(jnp.bfloat16)
                return carry

            lax.fori_loop(0, 2, body, 0)
            state[p] = push(
                own[w].at[z, 1 - x, rows, columns(y, width)],
                far[w].at[0, rows],
                p,
                depth + 1,
                site(core, 1 - x, z, y),
            )
            return

        def body(i, carry):
            mine = own[w].at[i, x, rows, columns(y, width)]
            mine[...] = add(mine, far[w].at[i, rows]).astype(jnp.bfloat16)
            return carry

        lax.fori_loop(0, depth, body, 0)
        state[p] = [
            push(
                own[w].at[lax.rem(z + k, depth), x, rows, columns(y, width)],
                last[w].at[k - 1, rows],
                p,
                k - 1,
                site(core, x, lax.rem(z + k, depth), y),
            )
            for k in range(1, depth)
        ]

    def stage4(p):
        w, rows, width, kind = view(p)
        if kind == 2:
            state[p].wait_recv()
            outs[w][rows] = add(own[w].at[z, x, rows, columns(y, width)], far[w].at[0, rows])
            return
        for copy in state[p]:
            copy.wait_recv()
        total = own[w][z, x, rows, columns(y, width)].astype(jnp.float32)
        for k in range(depth - 1):
            total = total + last[w][k, rows].astype(jnp.float32)
        outs[w][rows] = total

    in_steps(parts, (stage0, stage1, stage2, stage3, stage4), {1: 0, 2: 3, 3: 5, 4: 7})
    for copy in pending:
        copy.wait_send()


def reduce_sum(grads, pieces, cid, depth):
    count = len(grads)
    shapes = [(g.shape[0] // (4 * depth), g.shape[1] // 2) for g in grads]
    parts = split_rows(shapes, pieces)
    total = len(parts)

    def each(form):
        return [pltpu.VMEM(form(r, c), jnp.bfloat16) for r, c in shapes]

    return pl.pallas_call(
        functools.partial(reduce_kernel, parts, depth, count, shapes),
        in_specs=[pl.BlockSpec(memory_space=pl.ANY)] * count,
        out_specs=[pl.BlockSpec(memory_space=pltpu.VMEM)] * count,
        out_shape=[jax.ShapeDtypeStruct(s, jnp.float32) for s in shapes],
        scratch_shapes=each(lambda r, c: (depth, 2, r, 2 * c))
        + each(lambda r, c: (depth, 2, r, 2 * c))
        + each(lambda r, c: (depth, 2, r, c))
        + each(lambda r, c: (depth, r, 2 * c))
        + each(lambda r, c: (depth, r, c))
        + each(lambda r, c: (depth - 1, r, c))
        + [
            pltpu.VMEM((depth - 1, 2, r, 2 * c) if n == 0 else (8, LANES), jnp.bfloat16)
            for (r, c), n in zip(shapes, pieces)
        ]
        + [
            pltpu.SemaphoreType.DMA((total,)),
            pltpu.SemaphoreType.DMA((total, depth + 2)),
            pltpu.SemaphoreType.DMA((total, depth + 2)),
        ],
        compiler_params=pltpu.CompilerParams(
            collective_id=cid, has_side_effects=True, vmem_limit_bytes=56 * 1024 * 1024
        ),
    )(*[g.reshape(depth, 2, 2, r, 2 * c) for g, (r, c) in zip(grads, shapes)])


def general_body(
    images,
    cotangent,
    w_qkv,
    w_out,
    w_up,
    w_down,
    gains,
    biases,
    first_qkv,
    first_out,
    first_up,
    first_down,
    first_gains,
    first_biases,
    second_qkv,
    second_out,
    second_up,
    second_down,
    second_gains,
    second_biases,
):
    params = (w_qkv, w_out, w_up, w_down, gains, biases)
    firsts = (first_qkv, first_out, first_up, first_down, first_gains, first_biases)
    seconds = (second_qkv, second_out, second_up, second_down, second_gains, second_biases)
    count, group, width = images.shape
    ways = lax.axis_size("seq")
    blocks = lax.axis_size("dp")
    me = lax.axis_index("seq")
    pad_len = group * ways
    by_image = count % ways == 0
    rows_dp = w_qkv.shape[0]
    cols = w_out.shape[1]
    fold = w_up.shape[1] // cols
    own = gains.shape[1]
    small = jnp.concatenate([gains, biases], axis=0).astype(jnp.bfloat16).T
    lanes = -(-small.shape[1] // LANES) * LANES
    small = jnp.pad(small, ((0, rows_dp - own), (0, lanes - small.shape[1])))
    part_a = jnp.concatenate([w_qkv.astype(jnp.bfloat16), small], axis=1)
    wide_a = lax.all_gather(part_a, ("seq", "dp"), axis=0, tiled=True)
    part_b = jnp.concatenate(
        [
            w_out.astype(jnp.bfloat16),
            w_up.astype(jnp.bfloat16)
            .reshape(rows_dp, fold, cols)
            .transpose(1, 0, 2)
            .reshape(fold * rows_dp, cols),
            w_down.astype(jnp.bfloat16),
        ],
        axis=0,
    )
    part_b, wide_a = lax.optimization_barrier((part_b, wide_a))
    wide_b = lax.all_gather(part_b, ("seq", "dp"), axis=0, tiled=True)
    wide_a = wide_a.reshape(ways, width, part_a.shape[1])
    wide_qkv = jnp.concatenate([wide_a[k, :, : w_qkv.shape[1]] for k in range(ways)], axis=1)
    wide_small = (
        wide_a.reshape(ways, blocks, rows_dp, part_a.shape[1])[
            :, :, :own, w_qkv.shape[1] : w_qkv.shape[1] + 12
        ]
        .astype(jnp.float32)
        .transpose(3, 1, 0, 2)
        .reshape(12, width)
    )
    gain, bias = wide_small[:2], wide_small[2:]
    back_gain = gain
    wide_b = wide_b.reshape(ways, blocks, part_b.shape[0], cols)
    wide_out = wide_b[:, :, :rows_dp].transpose(1, 2, 0, 3).reshape(width, width)
    wide_up = (
        wide_b[:, :, rows_dp : (1 + fold) * rows_dp]
        .reshape(ways, blocks, fold, rows_dp, cols)
        .transpose(1, 3, 0, 2, 4)
        .reshape(width, fold * width)
    )
    wide_down = (
        wide_b[:, :, (1 + fold) * rows_dp :].transpose(1, 2, 0, 3).reshape(fold * width, width)
    )
    back_qkv, back_out, back_up, back_down = wide_qkv, wide_out, wide_up, wide_down
    spot = jnp.arange(group, dtype=jnp.int32)
    if by_image:
        images, cotangent = spread(images), spread(cotangent)
        token_live = jnp.concatenate(
            [lax.rem(me - k + ways, ways) * group + spot for k in range(ways)]
        ) < PATCH_TOK
        key_live = token_live
    else:
        token_live = me * group + spot < PATCH_TOK
        key_live = jnp.arange(pad_len, dtype=jnp.int32) < PATCH_TOK
    query_live = token_live
    key_live = key_live.astype(jnp.float32)
    rows = images.astype(jnp.float32)
    normed_a, inverse_a = normalize(rows)
    hidden_a = (normed_a * gain[0] + bias[0]).astype(jnp.bfloat16)
    mixed = jnp.einsum("icd,de->ice", hidden_a, wide_qkv, preferred_element_type=jnp.float32)
    queries = (mixed[..., :width] + bias[1]).astype(jnp.bfloat16)
    keys = mixed[..., width : 2 * width].astype(jnp.bfloat16)
    values = (mixed[..., 2 * width :] + bias[2]).astype(jnp.bfloat16)
    if by_image:
        keys_all, values_all = keys, values
    else:
        keys_all, values_all = (
            lax.all_gather(keys, "seq", axis=1, tiled=True),
            lax.all_gather(values, "seq", axis=1, tiled=True),
        )
    context = attend(queries, keys_all, values_all, key_live)
    resid = (
        rows
        + jnp.einsum("icd,de->ice", context, wide_out, preferred_element_type=jnp.float32)
        + bias[3]
    )
    normed_b, inverse_b = normalize(resid)
    hidden_b = (normed_b * gain[1] + bias[4]).astype(jnp.bfloat16)
    pre = jnp.einsum("icd,df->icf", hidden_b, wide_up, preferred_element_type=jnp.float32) + bias[
        6:
    ].reshape(-1)
    active = gelu_value(pre).astype(jnp.bfloat16)
    out_images = (
        resid
        + jnp.einsum("icf,fd->icd", active, wide_down, preferred_element_type=jnp.float32)
        + bias[5]
    ).astype(jnp.bfloat16)
    grad_y = cotangent.astype(jnp.float32) * query_live[None, :, None].astype(jnp.float32)
    grad_yb = grad_y.astype(jnp.bfloat16)
    g_down = jnp.einsum("icf,icd->fd", active, grad_yb, preferred_element_type=jnp.float32)
    grad_pre = jnp.einsum(
        "icd,fd->icf", grad_yb, back_down, preferred_element_type=jnp.float32
    ) * gelu_slope(pre)
    grad_preb = grad_pre.astype(jnp.bfloat16)
    g_up = jnp.einsum("icd,icf->df", hidden_b, grad_preb, preferred_element_type=jnp.float32)
    grad_hb = jnp.einsum("icf,df->icd", grad_preb, back_up, preferred_element_type=jnp.float32)
    grad_resid = grad_y + norm_back(grad_hb, normed_b, inverse_b, back_gain[1])
    grad_rb = grad_resid.astype(jnp.bfloat16)
    g_outw = jnp.einsum("icd,ice->de", context, grad_rb, preferred_element_type=jnp.float32)
    grad_ctx = jnp.einsum(
        "ice,de->icd", grad_rb, back_out, preferred_element_type=jnp.float32
    ).astype(jnp.bfloat16)
    grad_q, grad_k, grad_v = attend_back(
        queries,
        keys_all,
        values_all,
        grad_ctx,
        key_live,
        jnp.float32 if by_image else jnp.bfloat16,
    )
    if not by_image:
        grad_k, grad_v = (
            lax.psum_scatter(grad_k, "seq", scatter_dimension=1, tiled=True).astype(jnp.float32),
            lax.psum_scatter(grad_v, "seq", scatter_dimension=1, tiled=True).astype(jnp.float32),
        )
    grad_mixed = jnp.concatenate([grad_q, grad_k, grad_v], axis=-1).astype(jnp.bfloat16)
    g_qkv = jnp.einsum("icd,ice->de", hidden_a, grad_mixed, preferred_element_type=jnp.float32)
    grad_ha = jnp.einsum("ice,de->icd", grad_mixed, back_qkv, preferred_element_type=jnp.float32)
    grad_images = (grad_resid + norm_back(grad_ha, normed_a, inverse_a, back_gain[0])).astype(
        jnp.bfloat16
    )
    g_gains = jnp.stack(
        [jnp.sum(grad_ha * normed_a, axis=(0, 1)), jnp.sum(grad_hb * normed_b, axis=(0, 1))]
    )
    g_biases = jnp.concatenate(
        [
            jnp.stack(
                [
                    jnp.sum(grad_ha, axis=(0, 1)),
                    jnp.sum(grad_q, axis=(0, 1)),
                    jnp.sum(grad_v, axis=(0, 1)),
                    jnp.sum(grad_resid, axis=(0, 1)),
                    jnp.sum(grad_hb, axis=(0, 1)),
                    jnp.sum(grad_y, axis=(0, 1)),
                ]
            ),
            jnp.sum(grad_pre, axis=(0, 1)).reshape(-1, width),
        ],
        axis=0,
    )
    if by_image:
        out_images, grad_images = unspread(out_images), unspread(grad_images)
    send_a = jnp.concatenate(
        [
            g_outw.astype(jnp.bfloat16).reshape(blocks, rows_dp, width),
            g_up.astype(jnp.bfloat16)
            .reshape(blocks, rows_dp, ways, fold, cols)
            .transpose(0, 3, 1, 2, 4)
            .reshape(blocks, fold * rows_dp, width),
            g_down.astype(jnp.bfloat16).reshape(blocks, fold * rows_dp, width),
        ],
        axis=1,
    ).reshape(-1, width)
    part = lax.psum_scatter(send_a, "dp", scatter_dimension=0, tiled=True)
    total_a = sum_over_seq(part, 1)
    g_small = jnp.concatenate([g_gains, g_biases], axis=0).astype(jnp.bfloat16).T
    g_small = jnp.pad(g_small, ((0, 0), (0, lanes - g_small.shape[1])))
    send_b = jnp.concatenate([g_qkv.astype(jnp.bfloat16), g_small], axis=1)
    part, _ = lax.optimization_barrier((send_b, part))
    part = lax.psum_scatter(part, "dp", scatter_dimension=0, tiled=True)
    total_qkv = sum_over_seq(part[:, : g_qkv.shape[1]], 1)
    total_small = sum_over_seq(part[:, g_qkv.shape[1] :], 0)[:, :12].T
    totals = (
        total_qkv,
        total_a[:rows_dp],
        total_a[rows_dp : (1 + fold) * rows_dp]
        .reshape(fold, rows_dp, cols)
        .transpose(1, 0, 2)
        .reshape(rows_dp, fold * cols),
        total_a[(1 + fold) * rows_dp :],
        total_small[:2],
        total_small[2:],
    )
    updated = [
        adamw(param, grad, first, second)
        for param, grad, first, second in zip(params, totals, firsts, seconds)
    ]
    news = tuple((entry[0] for entry in updated))
    new_firsts = tuple((entry[1] for entry in updated))
    new_seconds = tuple((entry[2] for entry in updated))
    return (
        out_images,
        grad_images,
        totals[0],
        totals[1],
        totals[2],
        totals[3],
        totals[4],
        totals[5],
        news[0],
        news[1],
        news[2],
        news[3],
        news[4],
        news[5],
        new_firsts[0],
        new_firsts[1],
        new_firsts[2],
        new_firsts[3],
        new_firsts[4],
        new_firsts[5],
        new_seconds[0],
        new_seconds[1],
        new_seconds[2],
        new_seconds[3],
        new_seconds[4],
        new_seconds[5],
    )


def is_paired(mesh):
    return mesh.shape["seq"] == 2 and mesh.shape["dp"] % 4 == 0


def head_lanes(rows):
    lane = lax.broadcasted_iota(jnp.int32, (rows, LANES), 1)
    return lane // HEAD_DIM, lax.rem(lane, HEAD_DIM)


def three_terms(spot, value):
    high = value.astype(jnp.bfloat16)
    rest = value - high.astype(jnp.float32)
    middle = rest.astype(jnp.bfloat16)
    low = (rest - middle.astype(jnp.float32)).astype(jnp.bfloat16)
    zero = jnp.zeros((), jnp.bfloat16)
    return jnp.where(
        spot == 0, high, jnp.where(spot == 1, middle, jnp.where(spot == 2, low, zero))
    )


def dead_lane(spot, live):
    floor = jnp.where(live > 0.5, 0.0, -1e30)
    ones = jnp.where(spot < 3, 1.0, jnp.where(spot == 3, floor, 0.0))
    return ones.astype(jnp.bfloat16)


def attend_mixed_kernel(q_ref, k_ref, v_ref, live_ref, ctx_ref, lse_ref):
    q, k, v = q_ref[0], k_ref[0], v_ref[0]
    half, spot = head_lanes(q.shape[0])
    q = q * jnp.asarray(HEAD_DIM**-0.5, q.dtype)
    side_q = (spot == 3).astype(jnp.float32).astype(jnp.bfloat16)
    side_k = dead_lane(spot, live_ref[...])
    total = jnp.zeros(q.shape, jnp.float32)
    lse = jnp.zeros(q.shape, jnp.float32)
    for h in range(LANES // HEAD_DIM):
        mask = half == h
        scores = dot(jnp.where(mask, q, side_q), jnp.where(mask, k, side_k), NT)
        top = jnp.max(scores, axis=-1, keepdims=True)
        weights = jnp.exp(scores - top)
        denom = jnp.sum(weights, axis=-1, keepdims=True)
        total = jnp.where(mask, dot(weights.astype(jnp.bfloat16), v, NN) * (1.0 / denom), total)
        lse = jnp.where(mask, lse, top + jnp.log(denom))
    ctx_ref[0] = total.astype(jnp.bfloat16)
    lse_ref[0] = lse


def mixed_specs(rows, heads):
    return [
        pl.BlockSpec((1, rows, LANES), lambda i, h, k=k: (i, 0, h + k * heads)) for k in range(3)
    ]


def attend_mixed(mixed, live):
    count, rows, triple = mixed.shape
    width = triple // 3
    heads = width // LANES
    specs = mixed_specs(rows, heads)
    pairs = count * rows * rows * width
    return pl.pallas_call(
        attend_mixed_kernel,
        grid=(count, heads),
        in_specs=specs + [pl.BlockSpec((rows, 1), lambda i, h: (0, 0))],
        out_specs=[specs[0], specs[0]],
        out_shape=[
            jax.ShapeDtypeStruct((count, rows, width), jnp.bfloat16),
            jax.ShapeDtypeStruct((count, rows, width), jnp.float32),
        ],
        cost_estimate=pl.CostEstimate(
            flops=8 * pairs, bytes_accessed=2 * mixed.size, transcendentals=pairs // HEAD_DIM
        ),
        compiler_params=pltpu.CompilerParams(vmem_limit_bytes=48 * 1024 * 1024),
    )(mixed, mixed, mixed, live.reshape(rows, 1))


def attend_back_mixed_kernel(
    q_ref, k_ref, v_ref, g_ref, ctx_ref, lse_ref, live_ref, dm_ref, sum_ref
):
    q, k, v, g = q_ref[0], k_ref[0], v_ref[0], g_ref[0]
    scale = HEAD_DIM**-0.5
    half, spot = head_lanes(q.shape[0])
    q = q * jnp.asarray(scale, q.dtype)
    one = (spot == 3).astype(jnp.float32).astype(jnp.bfloat16)
    side_q = three_terms(spot, -lse_ref[0]) + one
    side_k = dead_lane(spot, live_ref[...])
    side_v = (spot < 3).astype(jnp.float32).astype(jnp.bfloat16)
    agree = g.astype(jnp.float32) * ctx_ref[0].astype(jnp.float32)
    dq = jnp.zeros(q.shape, jnp.float32)
    dk = jnp.zeros(q.shape, jnp.float32)
    dv = jnp.zeros(q.shape, jnp.float32)
    for h in range(LANES // HEAD_DIM):
        mask = half == h
        delta = jnp.sum(jnp.where(mask, agree, 0.0), axis=1, keepdims=True)
        q_h = jnp.where(mask, q, side_q)
        k_h = jnp.where(mask, k, side_k)
        v_h = jnp.where(mask, v, side_v)
        g_h = jnp.where(mask, g, three_terms(spot, jnp.broadcast_to(-delta, q.shape)))
        probs = jnp.exp(dot(k_h, q_h, NT))
        grad_scores = (probs * dot(v_h, g_h, NT)).astype(jnp.bfloat16)
        dv = jnp.where(mask, dot(probs.astype(jnp.bfloat16), g, NN), dv)
        dk = jnp.where(mask, dot(grad_scores, q, NN), dk)
        dq = jnp.where(mask, dot(grad_scores, k, TN), dq)
    image, head = pl.program_id(0), pl.program_id(1)
    width = dm_ref.shape[2] // 3

    @pl.when(jnp.logical_and(image == 0, head == 0))
    def _():
        sum_ref[...] = jnp.zeros_like(sum_ref)

    for n, part in enumerate((dq * scale, dk, dv)):
        where = pl.ds(pl.multiple_of(n * width + head * LANES, LANES), LANES)
        dm_ref[0, :, where] = part.astype(jnp.bfloat16)
        sum_ref[:, where] += jnp.sum(part, axis=0, keepdims=True)


def attend_back_mixed(mixed, grad_ctx, context, lse, live):
    count, rows, triple = mixed.shape
    width = triple // 3
    heads = width // LANES
    specs = mixed_specs(rows, heads)
    pairs = count * rows * rows * width
    return pl.pallas_call(
        attend_back_mixed_kernel,
        grid=(count, heads),
        in_specs=specs + [specs[0]] * 3 + [pl.BlockSpec((rows, 1), lambda i, h: (0, 0))],
        out_specs=[
            pl.BlockSpec((1, rows, triple), lambda i, h: (i, 0, 0)),
            pl.BlockSpec((1, triple), lambda i, h: (0, 0)),
        ],
        out_shape=[
            jax.ShapeDtypeStruct(mixed.shape, jnp.bfloat16),
            jax.ShapeDtypeStruct((1, triple), jnp.float32),
        ],
        cost_estimate=pl.CostEstimate(
            flops=20 * pairs, bytes_accessed=4 * mixed.size, transcendentals=pairs // HEAD_DIM
        ),
        compiler_params=pltpu.CompilerParams(vmem_limit_bytes=56 * 1024 * 1024),
    )(mixed, mixed, mixed, grad_ctx, context, lse, live.reshape(rows, 1))


def small_kernel(slots, own, lanes, *refs):
    rows, out_ref, stack = refs[:-2], refs[-2], refs[-1]
    stack[...] = jnp.zeros_like(stack)
    out_ref[...] = jnp.zeros_like(out_ref)
    width = stack.shape[1]
    at = 0
    for ref in rows:
        for start in range(0, ref.shape[1], width):
            stack[at : at + 1] = ref[:, start : start + width]
            at += 1
    filled = stack[...].astype(jnp.bfloat16)
    for slot in range(slots):
        piece = filled[:, slot * own : (slot + 1) * own]
        out_ref[slot // 2, :, (slot % 2) * lanes : (slot % 2) * lanes + own] = piece


def pack_small(rows, blocks, tall, own, lanes):
    width = rows[0].shape[1]
    return pl.pallas_call(
        functools.partial(small_kernel, 2 * blocks, own, lanes),
        out_shape=jax.ShapeDtypeStruct((blocks, tall, 2 * lanes), jnp.bfloat16),
        scratch_shapes=[pltpu.VMEM((tall, width), jnp.float32)],
    )(*rows).reshape(blocks * tall, 2 * lanes)


def product(a, b, dims=NN):
    return lax.dot_general(a, b, dims, preferred_element_type=jnp.float32)


def sum_rows(rows):
    return jnp.sum(rows, axis=0, keepdims=True)


def fast_body(images, cotangent, *rest):
    params, firsts, seconds = rest[:6], rest[6:12], rest[12:]
    w_qkv, w_out, w_up, w_down, gains, biases = params
    count, group, width = images.shape
    ways = lax.axis_size("seq")
    blocks = lax.axis_size("dp")
    depth = blocks // 4
    me = lax.axis_index("seq")
    narrow = jnp.bfloat16
    vectors = gains.shape[0] + biases.shape[0]
    own = gains.shape[1]
    lanes = -(-own // LANES) * LANES
    tall = -(-vectors // 32) * 32
    small = jnp.concatenate([gains, biases], axis=0).astype(narrow)
    small = jnp.pad(small, ((0, tall - vectors), (0, lanes - own)))
    images, cotangent = spread(images), spread(cotangent)
    each, length = images.shape[:2]
    wide_qkv, wide_small, wide_out, wide_up, wide_down = gather(
        [w_qkv.astype(narrow), small, w_out.astype(narrow), w_up.astype(narrow), w_down.astype(narrow)],
        (4, 2, 2, 4, 0),
        1,
        depth,
    )
    wide_small = (
        wide_small.reshape(blocks, tall, ways, lanes)[:, :vectors, :, :own]
        .astype(jnp.float32)
        .transpose(1, 0, 2, 3)
        .reshape(vectors, width)
    )
    gain, bias = wide_small[: gains.shape[0]], wide_small[gains.shape[0] :]
    spot = jnp.arange(group, dtype=jnp.int32)
    live = jnp.concatenate(
        [lax.rem(me - k + ways, ways) * group + spot for k in range(ways)]
    ) < PATCH_TOK
    key_live = live.astype(jnp.float32)
    rows = images.reshape(each * length, width).astype(jnp.float32)
    normed_a, inverse_a = normalize(rows)
    hidden_a = (normed_a * gain[0] + bias[0]).astype(narrow)
    shift = jnp.concatenate([bias[1], jnp.zeros_like(bias[1]), bias[2]])
    mixed = (product(hidden_a, wide_qkv) + shift).astype(narrow).reshape(each, length, 3 * width)
    context, lse = attend_mixed(mixed, key_live)
    context = context.reshape(each * length, width)
    resid = rows + product(context, wide_out) + bias[3]
    normed_b, inverse_b = normalize(resid)
    hidden_b = (normed_b * gain[1] + bias[4]).astype(narrow)
    pre = product(hidden_b, wide_up) + bias[6:].reshape(-1)
    active = gelu_value(pre).astype(narrow)
    out_images = (resid + product(active, wide_down) + bias[5]).astype(narrow)
    grad_y = cotangent.astype(jnp.float32) * live[None, :, None].astype(jnp.float32)
    grad_y = grad_y.reshape(each * length, width)
    grad_yb = grad_y.astype(narrow)
    grad_yb, out_images = lax.optimization_barrier((grad_yb, out_images))
    out_images = unspread(out_images.reshape(each, length, width))
    g_down = product(active, grad_yb, TN)
    grad_pre = product(grad_yb, wide_down, NT) * gelu_slope(pre)
    grad_preb = grad_pre.astype(narrow)
    g_up = product(hidden_b, grad_preb, TN)
    grad_hb = product(grad_preb, wide_up, NT)
    grad_resid = grad_y + norm_back(grad_hb, normed_b, inverse_b, gain[1])
    grad_rb = grad_resid.astype(narrow)
    g_outw = product(context, grad_rb, TN)
    grad_ctx = product(grad_rb, wide_out, NT).astype(narrow).reshape(each, length, width)
    grad_mixed, mixed_sum = attend_back_mixed(
        mixed, grad_ctx, context.reshape(each, length, width), lse, key_live
    )
    grad_mixed = grad_mixed.reshape(each * length, 3 * width)
    g_qkv = product(hidden_a, grad_mixed, TN)
    grad_ha = product(grad_mixed, wide_qkv, NT)
    grad_images = (grad_resid + norm_back(grad_ha, normed_a, inverse_a, gain[0])).astype(narrow)
    grad_images = unspread(grad_images.reshape(each, length, width))
    g_small = pack_small(
        [
            sum_rows(grad_ha * normed_a),
            sum_rows(grad_hb * normed_b),
            sum_rows(grad_ha),
            mixed_sum[:, :width],
            mixed_sum[:, 2 * width :],
            sum_rows(grad_resid),
            sum_rows(grad_hb),
            sum_rows(grad_y),
            sum_rows(grad_pre),
        ],
        blocks,
        tall,
        own,
        lanes,
    )
    t_down, t_up, t_out, t_qkv, t_small = reduce_sum(
        [g.astype(narrow) for g in (g_down, g_up, g_outw, g_qkv, g_small)],
        (0, 4, 2, 4, 2),
        2,
        depth,
    )
    t_small = t_small[:vectors, :own]
    totals = (t_qkv, t_out, t_up, t_down, t_small[: gains.shape[0]], t_small[gains.shape[0] :])
    updated = [
        adamw(param, grad, first, second)
        for param, grad, first, second in zip(params, totals, firsts, seconds)
    ]
    return (
        out_images,
        grad_images,
        *totals,
        *(entry[0] for entry in updated),
        *(entry[1] for entry in updated),
        *(entry[2] for entry in updated),
    )


def solution(mesh):
    body = fast_body if is_paired(mesh) else general_body
    return jax.shard_map(
        body,
        mesh=mesh,
        in_specs=(
            P("dp", "seq", None),
            P("dp", "seq", None),
            P("dp", "seq"),
            P("dp", "seq"),
            P("dp", "seq"),
            P("dp", "seq"),
            P(None, ("dp", "seq")),
            P(None, ("dp", "seq")),
            P("dp", "seq"),
            P("dp", "seq"),
            P("dp", "seq"),
            P("dp", "seq"),
            P(None, ("dp", "seq")),
            P(None, ("dp", "seq")),
            P("dp", "seq"),
            P("dp", "seq"),
            P("dp", "seq"),
            P("dp", "seq"),
            P(None, ("dp", "seq")),
            P(None, ("dp", "seq")),
        ),
        out_specs=(
            P("dp", "seq", None),
            P("dp", "seq", None),
            P("dp", "seq"),
            P("dp", "seq"),
            P("dp", "seq"),
            P("dp", "seq"),
            P(None, ("dp", "seq")),
            P(None, ("dp", "seq")),
            P("dp", "seq"),
            P("dp", "seq"),
            P("dp", "seq"),
            P("dp", "seq"),
            P(None, ("dp", "seq")),
            P(None, ("dp", "seq")),
            P("dp", "seq"),
            P("dp", "seq"),
            P("dp", "seq"),
            P("dp", "seq"),
            P(None, ("dp", "seq")),
            P(None, ("dp", "seq")),
            P("dp", "seq"),
            P("dp", "seq"),
            P("dp", "seq"),
            P("dp", "seq"),
            P(None, ("dp", "seq")),
            P(None, ("dp", "seq")),
        ),
        check_vma=False,
    )
```
